32 devices in a mesh: req: 8 (over z, x), tp: 4 (over y, core).
Axes of the slice: x: 2, y: 2, z: 4, core: 2. Of those that a mesh axis runs over, the one named last changes fastest.
Arguments:
- tokens: bfloat16 [4096, 3584], P('req'), may hold values from -400 to 400, as said below
- norm_gain: float32 [3584], P(('req', 'tp')), may hold values from 0.5 to 1.5
- qkv_weight: float32 [3584, 4608], P(('req', 'tp')), may hold values from -0.09375 to 0.09375
- qkv_bias: float32 [4608], P(('req', 'tp')), may hold values from -48 to 48
- lengths: int32 [8, 4], P('req'), may hold values from 1 to 256, 512 in all within a row
Outputs:
- context: bfloat16 [4096, 3584], P('req', 'tp')
The draws below stay inside these ranges and needn't reach their ends.
Inputs may be any that keep to these rules, and one draw needn't show every extreme that they name: `tokens`: hidden states of order one to some hundreds. Each replica's tenant lengths sum to 512, the largest is exactly 256.
All inputs are finite; a program needn't handle non-finite values.
Results may differ from the reference program's by a relative error of at most 0.009.
The reference program's roundings to bfloat16 on the way count: a program that leaves them out, or rounds other values in their place, can miss the bound.
Values may be sent and summed in bfloat16 or wider, within the bound.
A program may use at most 128 MiB of HBM per device.

```python
import math
import jax
import jax.numpy as jnp
import numpy as np
from jax import lax

D = 3584
HEADS = 28
HEAD_DIM = 128
TOK_DEV = 512
TENANTS = 4
SINKS = 4
GROUP = 7
QKV = 4608
MOST = 256
WINDOW = 160
TOKENS = 4096
N_REQ = 8


def draw_tokens(key, part):
    first, second, third = jax.random.split(key, 3)
    base = jnp.clip(jax.random.normal(first, (TOKENS, D), jnp.float32), -4.0, 4.0)
    rows = jnp.exp(jax.random.uniform(second, (TOKENS, 1), jnp.float32, 0.0, math.log(10.0)))
    cols = jnp.exp(jax.random.uniform(third, (1, D), jnp.float32, 0.0, math.log(10.0)))
    return (base * rows * cols).astype(jnp.bfloat16)


def draw_qkv_bias(key, part):
    first = jax.random.fold_in(key, 0)
    return jnp.clip(0.5 * jax.random.normal(first, (QKV,), jnp.float32), -2.0, 2.0)


def block_levels(stream_key, dims, pieces, low, top_value):
    loudness, own = 1.0, jax.random.fold_in(stream_key, 6)
    for axis_at, shards_of in pieces:
        steps = jnp.exp(jax.random.uniform(jax.random.fold_in(own, axis_at), (shards_of,), jnp.float32, low / len(pieces), top_value / len(pieces)))
        loudness = loudness * jnp.repeat(steps, dims[axis_at] // shards_of).reshape([-1 if axis == axis_at else 1 for axis in range(len(dims))])
    return loudness


def length_profile(number_of, total, limit, skew):
    weights = [(1 << 20) // math.isqrt(grade ** skew) + 1 for grade in range(2, number_of + 1)]
    rest, counts = total - limit - (number_of - 1), [1] * (number_of - 1)
    while rest > 0:
        candidates = [i for i in range(number_of - 1) if counts[i] < limit]
        mass, left = sum([weights[i] for i in candidates]), rest
        for i in candidates:
            more = min(limit - counts[i], max(1, left * weights[i] // mass), rest)
            counts[i] = counts[i] + more
            rest = rest - more
    return np.array([limit] + counts)


def ragged(stream_key, count, total, limit, skew):
    if count == 2:
        one = jax.random.randint(stream_key, (), max(1, total - limit), min(limit, total - 1) + 1)
        return jnp.stack([one, total - one])
    sizes = jnp.asarray(length_profile(count, total, limit, skew), jnp.int32)
    twos = (count - 1) // 2
    giver, taker = sizes[1:1 + 2 * twos:2], sizes[2:2 + 2 * twos:2]
    slack = jnp.minimum(giver - 1, limit - taker)
    passed = jax.random.randint(jax.random.fold_in(stream_key, 1), (twos,), 0, 1 << 20) % (slack + 1)
    sizes = sizes.at[1:1 + 2 * twos:2].set(giver - passed).at[2:2 + 2 * twos:2].set(taker + passed)
    return sizes[jax.random.permutation(jax.random.fold_in(stream_key, 2), count)]


def scatter_about(key, extent, spread, limit, shards=(), kind=jnp.bfloat16):
    drawn = spread * jax.random.normal(key, extent, jnp.float32)
    if shards:
        drawn = drawn * block_levels(key, extent, shards, -0.22, 0.18)
    return jnp.clip(drawn, -limit, limit).astype(kind)


def setup_inputs(seed: int = 0) -> dict:
    key_of = jax.random.split(jax.random.key(seed), 6)
    return {
        "tokens": draw_tokens(jax.random.fold_in(key_of[5], 71), 0),
        "norm_gain": jnp.clip(1.0 + 0.1 * jax.random.normal(key_of[1], (D,), jnp.float32), 0.5, 1.5),
        "qkv_weight": scatter_about(key_of[2], (D, QKV), D ** -0.5, 0.09375, ((0, 32),), jnp.float32),
        "qkv_bias": draw_qkv_bias(jax.random.fold_in(key_of[5], 71), 0),
        "lengths": jax.vmap(lambda own: ragged(own, TENANTS, TOK_DEV, MOST, 2))(jax.random.split(key_of[4], N_REQ)).reshape((N_REQ, TENANTS)).astype(jnp.int32),
    }


def normalize(values, gain):
    wide = values.astype(jnp.float32)
    meansq = lax.optimization_barrier(jnp.mean(wide * wide, axis=-1, keepdims=True))
    return (wide * lax.rsqrt(meansq + 1e-06) * gain.astype(jnp.float32)).astype(jnp.bfloat16)

def positions(lens, count):
    index = jnp.arange(count, dtype=jnp.int32)
    ends = jnp.cumsum(lens).astype(jnp.int32)
    after = index[:, None] >= ends[None, :]
    tenant = lax.optimization_barrier(jnp.sum(after.astype(jnp.int32), axis=1)).astype(jnp.int32)
    start = lax.optimization_barrier(jnp.sum(jnp.where(after, lens[None, :], 0), axis=1)).astype(jnp.int32)
    return (tenant, index - start)

def rotate(values, pos):
    half = HEAD_DIM // 2
    freqs = jnp.exp(-(jnp.arange(half, dtype=jnp.float32) * 2.0 / HEAD_DIM) * math.log(1000000.0))
    angle = pos.astype(jnp.float32)[:, None] * freqs[None, :]
    cosine = jnp.concatenate([jnp.cos(angle), jnp.cos(angle)], axis=-1)
    sine = jnp.concatenate([jnp.sin(angle), jnp.sin(angle)], axis=-1)
    shape = (values.shape[0],) + (1,) * (values.ndim - 2) + (HEAD_DIM,)
    cosine = cosine.reshape(shape)
    sine = sine.reshape(shape)
    turned = jnp.concatenate([-values[..., half:], values[..., :half]], axis=-1)
    return values * cosine + turned * sine

def attend(joined, tenant, pos):
    count = joined.shape[0]
    blocks = joined.reshape(count, -1, GROUP + 2, HEAD_DIM)
    query = rotate(blocks[:, :, :GROUP], pos).astype(jnp.bfloat16)
    key_part = rotate(blocks[:, :, GROUP], pos).astype(jnp.bfloat16)
    value_part = blocks[:, :, GROUP + 1].astype(jnp.bfloat16)
    scores = jnp.einsum('qghd,kgd->ghqk', query.astype(jnp.float32), key_part.astype(jnp.float32)) / math.sqrt(HEAD_DIM)
    same = tenant[:, None] == tenant[None, :]
    causal = pos[None, :] <= pos[:, None]
    near = jnp.logical_or(pos[:, None] - pos[None, :] < WINDOW, pos[None, :] < SINKS)
    allowed = jnp.logical_and(jnp.logical_and(same, causal), near)
    scores = jnp.where(allowed[None, None], scores, -1e+30)
    peak = lax.optimization_barrier(jnp.max(scores, axis=-1, keepdims=True))
    expo = jnp.where(allowed[None, None], jnp.exp(scores - peak), 0.0)
    weights = (expo / lax.optimization_barrier(jnp.sum(expo, axis=-1, keepdims=True))).astype(jnp.bfloat16)
    mixed = jnp.einsum('ghqk,kgd->qghd', weights.astype(jnp.float32), value_part.astype(jnp.float32))
    return mixed.reshape(count, -1).astype(jnp.bfloat16)

def reference(tokens, norm_gain, qkv_weight, qkv_bias, lengths):
    gain_b = norm_gain.astype(jnp.bfloat16)
    weight_b = qkv_weight.astype(jnp.bfloat16)
    bias_f = qkv_bias.astype(jnp.bfloat16).astype(jnp.float32)
    stacked = tokens.reshape(N_REQ, TOK_DEV, D)

    def replica(items):
        rows, lens = items
        normed = normalize(rows, gain_b)
        joined = jnp.dot(normed, weight_b, preferred_element_type=jnp.float32) + bias_f[None, :]
        tenant, pos = positions(lens, TOK_DEV)
        return attend(joined, tenant, pos)
    out = lax.map(replica, (stacked, lengths))
    return out.reshape(TOKENS, HEADS * HEAD_DIM)
```

```python
import functools
import math

import jax
import jax.numpy as jnp
from jax import lax
from jax.experimental import pallas as pl
from jax.experimental.pallas import tpu as pltpu
from jax.sharding import PartitionSpec as P

HEAD_DIM = 128
SINKS = 4
GROUP = 7
WINDOW = 160
MOST = 256
MESH = pl.DeviceIdType.MESH


def normalize(values, gain):
    wide = values.astype(jnp.float32)
    meansq = jnp.mean(wide * wide, axis=-1, keepdims=True)
    return (wide * lax.rsqrt(meansq + 1e-06) * gain.astype(jnp.float32)).astype(jnp.bfloat16)


def starts(lens, count):
    index = jnp.arange(count, dtype=jnp.int32)
    after = index[:, None] >= jnp.cumsum(lens)[None, :]
    return jnp.sum(jnp.where(after, lens[None, :], 0), axis=1)


def tables(lens, count):
    half = HEAD_DIM // 2
    pos = jnp.arange(count, dtype=jnp.int32) - starts(lens, count)
    freqs = jnp.exp(-(jnp.arange(half, dtype=jnp.float32) * 2.0 / HEAD_DIM) * math.log(1000000.0))
    angle = pos.astype(jnp.float32)[:, None] * freqs[None, :]
    cosine, sine = jnp.cos(angle), jnp.sin(angle)
    return (
        jnp.concatenate([cosine, cosine], axis=-1),
        jnp.concatenate([-sine, sine], axis=-1),
    )


def attend_kernel(lens_ref, joined_ref, cos_ref, sin_ref, out_ref):
    count = joined_ref.shape[0]
    tenants = lens_ref.shape[1]
    block = 128

    def turned(lo, size, column):
        v = joined_ref[lo : lo + size, column * HEAD_DIM : (column + 1) * HEAD_DIM]
        r = v * cos_ref[lo : lo + size, :] + pltpu.roll(v, HEAD_DIM // 2, 1) * sin_ref[lo : lo + size, :]
        return r.astype(jnp.bfloat16)

    keys = [turned(lo, block, GROUP) for lo in range(0, count, block)]
    values = joined_ref[:, (GROUP + 1) * HEAD_DIM :].astype(jnp.bfloat16)
    back = -(-(MOST - 1) // block)
    for at in range(count // block):
        first = max(0, at - back)
        wide = (at + 1 - first) * block
        query_at = at * block + lax.broadcasted_iota(jnp.int32, (block, 1), 0)
        key_at = first * block + lax.broadcasted_iota(jnp.int32, (block, wide), 1)
        start = jnp.zeros((block, 1), jnp.int32)
        end = jnp.int32(0)
        for t in range(tenants):
            end = end + lens_ref[0, t]
            start = jnp.where(query_at >= end, end, start)
        low = jnp.maximum(query_at - (WINDOW - 1), start)
        allowed = jnp.logical_and(
            key_at <= query_at,
            jnp.logical_or(
                key_at >= low, jnp.logical_and(key_at >= start, key_at < start + SINKS)
            ),
        )
        key_block = jnp.concatenate(keys[first : at + 1], axis=0)
        value_block = values[first * block : (at + 1) * block]
        for head in range(GROUP):
            query = turned(at * block, block, head)
            scores = lax.dot_general(
                query, key_block, (((1,), (1,)), ((), ())), preferred_element_type=jnp.float32
            ) * (1.0 / math.sqrt(HEAD_DIM))
            scores = jnp.where(allowed, scores, -1e30)
            peak = jnp.max(scores, axis=-1, keepdims=True)
            expo = jnp.exp(scores - peak)
            weights = (expo * (1.0 / jnp.sum(expo, axis=-1, keepdims=True))).astype(jnp.bfloat16)
            mixed = jnp.dot(weights, value_block, preferred_element_type=jnp.float32)
            out_ref[at * block : (at + 1) * block, head * HEAD_DIM : (head + 1) * HEAD_DIM] = (
                mixed.astype(jnp.bfloat16)
            )


def attend(joined, lens):
    count = joined.shape[0]
    cosine, sine = tables(lens[0], count)
    vmem = pl.BlockSpec(memory_space=pltpu.VMEM)
    return pl.pallas_call(
        attend_kernel,
        out_shape=jax.ShapeDtypeStruct((count, GROUP * HEAD_DIM), jnp.bfloat16),
        in_specs=[pl.BlockSpec(memory_space=pltpu.SMEM), vmem, vmem, vmem],
        out_specs=vmem,
        compiler_params=pltpu.CompilerParams(vmem_limit_bytes=32 << 20),
        name="attention",
    )(lens, joined, cosine, sine)


def project_kernel(
    w_ref, side_ref, tok_hbm, out_ref,
    wb, full, tok, normed, scale, sides, tok_sem,
    first_send, first_recv, side_send, side_recv,
    ring_send, ring_recv, trail_send, trail_recv,
):
    req, tp = lax.axis_index("req"), lax.axis_index("tp")
    count, depth = tok.shape
    shard, width = full.shape[1:]
    z, x = req // 2, req % 2
    y, core = tp // 2, tp % 2
    place = (1 - x) * z + x * (7 - z)

    def req_at(pos):
        pos = pos % 8
        far = pos // 4
        return (1 - far) * (2 * pos) + far * (2 * (7 - pos) + 1)

    right, left = req_at(place + 1), req_at(place + 7)
    peers = (2 * y + 1 - core, 2 * (1 - y) + core, 2 * (1 - y) + 1 - core)
    own = 4 * req + tp

    tok_copy = pltpu.make_async_copy(tok_hbm, tok, tok_sem)
    tok_copy.start()

    barrier = pltpu.get_barrier_semaphore()
    for peer in peers:
        pl.semaphore_signal(barrier, inc=1, device_id=(req, peer), device_id_type=MESH)
    for near in (left, right):
        pl.semaphore_signal(barrier, inc=1, device_id=(near, tp), device_id_type=MESH)

    def columns(t):
        return w_ref[:, pl.ds(pl.multiple_of(t * width, 128), width)].astype(jnp.bfloat16)

    wb[0] = columns(peers[0])
    full[own] = columns(tp)
    sides[own] = side_ref[...]
    pl.semaphore_wait(barrier, 5)

    firsts, side_firsts = [], []
    for k, peer in enumerate(peers):
        if k:
            wb[k] = columns(peer)
        copy = pltpu.make_async_remote_copy(
            src_ref=wb.at[k], dst_ref=full.at[own],
            send_sem=first_send.at[k], recv_sem=first_recv.at[k],
            device_id=(req, peer), device_id_type=MESH,
        )
        copy.start()
        firsts.append(copy)
    for k, peer in enumerate(peers):
        copy = pltpu.make_async_remote_copy(
            src_ref=side_ref, dst_ref=sides.at[own],
            send_sem=side_send.at[k], recv_sem=side_recv.at[k],
            device_id=(req, peer), device_id_type=MESH,
        )
        copy.start()
        side_firsts.append(copy)

    ring = {}
    trail = {}

    def send(way, hop, piece):
        source = req_at(place + 8 - hop) if way == 0 else req_at(place + hop)
        row = y if piece == 0 else 1 - y
        slot = 4 * source + 2 * row + way
        copy = pltpu.make_async_remote_copy(
            src_ref=full.at[slot], dst_ref=full.at[slot],
            send_sem=ring_send.at[way, hop, piece], recv_sem=ring_recv.at[way, hop, piece],
            device_id=(right if way == 0 else left, tp), device_id_type=MESH,
        )
        copy.start()
        ring[way, hop, piece] = copy

    def send_trail(hop):
        rows = pl.ds(4 * req_at(place + 8 - hop), 4)
        copy = pltpu.make_async_remote_copy(
            src_ref=sides.at[rows], dst_ref=sides.at[rows],
            send_sem=trail_send.at[hop], recv_sem=trail_recv.at[hop],
            device_id=(right, tp), device_id_type=MESH,
        )
        copy.start()
        trail[hop] = copy

    def spread(row, parts, step):
        total = step * len(parts)
        line = jnp.zeros((8, total), jnp.float32)
        for i, part in enumerate(parts):
            have = part.shape[1]
            padded = jnp.concatenate([part, jnp.zeros((8, total - have), jnp.float32)], axis=1)
            line = line + (pltpu.roll(padded, step * i, 1) if i else padded)
        return line[row : row + 1, :]

    group = depth // 4

    def chunk(c, begin, bias):
        gain = spread(0, [sides[8 * c + i] for i in range(8)], shard)
        offset = pl.multiple_of(c * group, 128)

        @pl.loop(0, count // 64)
        def _(i):
            rows = pl.ds(pl.multiple_of(i * 64, 64), 64)
            wide = tok[rows, pl.ds(offset, group)].astype(jnp.float32)
            normed[rows, :] = (wide * scale[rows, :][:, :1] * gain).astype(jnp.bfloat16)

        for n in range(3):
            part = width // 3
            lo = n * part
            block = full[pl.ds(8 * c, 8), :, lo : lo + part].reshape(group, part)
            product = jnp.dot(normed[...], block, preferred_element_type=jnp.float32)
            if begin:
                out_ref[:, lo : lo + part] = product
            elif bias is None:
                out_ref[:, lo : lo + part] += product
            else:
                out_ref[:, lo : lo + part] += product + bias[:, lo : lo + part]

    inner = (z % 3 + 2) // 3
    order0 = inner * z + (1 - inner) * (3 - z)
    order1 = (z + 2) % 4
    order2 = (z * 3) // 4
    order3 = 6 - order0 - order1 - order2

    for step in range(8):
        for way in range(2):
            if step == 0 and way == 0:
                firsts[0].wait_recv()
            if step >= 1:
                ring[way, step - 1, 0].wait_recv()
            if step <= 6:
                send(way, step, 0)
        if step >= 1:
            for way in range(2):
                if step == 1 and way == 0:
                    firsts[1].wait_recv()
                    firsts[2].wait_recv()
                if step >= 2:
                    ring[way, step - 2, 1].wait_recv()
                send(way, step - 1, 1)
            if step == 1:
                for copy in side_firsts:
                    copy.wait_recv()
            else:
                trail[step - 2].wait_recv()
            send_trail(step - 1)
        if step == 0:
            tok_copy.wait()

            @pl.loop(0, count // 32)
            def _(i):
                rows = pl.ds(pl.multiple_of(i * 32, 32), 32)
                wide = tok[rows, :].astype(jnp.float32)
                mean = jnp.sum(wide * wide, axis=-1, keepdims=True) * (1.0 / depth)
                scale[rows, :] = jnp.broadcast_to(lax.rsqrt(mean + 1e-06), (32, 128))
        elif step == 6:
            chunk(order0, True, None)
        elif step == 7:
            chunk(order1, False, None)
    for way in range(2):
        ring[way, 6, 1].wait_recv()
    trail[6].wait_recv()
    bias = spread_bias(sides, tp, width)
    chunk(order2, False, None)
    chunk(order3, False, bias)
    for copy in firsts + side_firsts + list(ring.values()) + list(trail.values()):
        copy.wait_send()


def spread_bias(sides, tp, width):
    step = width // 8
    line = jnp.zeros((8, width), jnp.float32)
    for i in range(8):
        both = sides[8 * tp + i]
        head = pltpu.roll(both, 7, 0)
        tail = pltpu.roll(both, 6, 0)
        padded = jnp.concatenate([head, tail, jnp.zeros((8, width - 256), jnp.float32)], axis=1)
        line = line + (pltpu.roll(padded, step * i, 1) if i else padded)
    return line[0:1, :]


def project(tokens, norm_gain, qkv_weight, qkv_bias):
    count, depth = tokens.shape
    shard, total = qkv_weight.shape
    width = total // 4
    line = lambda v, size: jnp.pad(v.astype(jnp.bfloat16).astype(jnp.float32), (0, size - v.shape[0]))
    side = jnp.concatenate([line(norm_gain, 128), line(qkv_bias, 896)]).reshape(8, 128)
    vmem = pl.BlockSpec(memory_space=pltpu.VMEM)
    dma = pltpu.SemaphoreType.DMA
    return pl.pallas_call(
        project_kernel,
        out_shape=jax.ShapeDtypeStruct((count, width), jnp.float32),
        in_specs=[vmem, vmem, pl.BlockSpec(memory_space=pl.ANY)],
        out_specs=vmem,
        scratch_shapes=[
            pltpu.VMEM((3, shard, width), jnp.bfloat16),
            pltpu.VMEM((32, shard, width), jnp.bfloat16),
            pltpu.VMEM((count, depth), jnp.bfloat16),
            pltpu.VMEM((count, depth // 4), jnp.bfloat16),
            pltpu.VMEM((count, 128), jnp.float32),
            pltpu.VMEM((32, 8, 128), jnp.float32),
            dma,
            dma((3,)), dma((3,)), dma((3,)), dma((3,)),
            dma((2, 7, 2)), dma((2, 7, 2)), dma((7,)), dma((7,)),
        ],
        compiler_params=pltpu.CompilerParams(
            collective_id=0, has_side_effects=True, vmem_limit_bytes=48 << 20
        ),
        name="project",
    )(qkv_weight, side, tokens)


def project_plain(tokens, norm_gain, qkv_weight, qkv_bias):
    tp_count = lax.axis_size("tp")
    req_count = lax.axis_size("req")
    tp_place = lax.axis_index("tp")
    gain_full, bias_full = (
        lax.all_gather(norm_gain.astype(jnp.bfloat16), ("req", "tp"), axis=0, tiled=True),
        lax.all_gather(qkv_bias.astype(jnp.bfloat16), ("req", "tp"), axis=0, tiled=True),
    )
    width = bias_full.shape[0] // tp_count
    bias_block = lax.dynamic_slice_in_dim(bias_full, tp_place * width, width).astype(jnp.float32)
    normed = normalize(tokens, gain_full)
    weight_b = qkv_weight.astype(jnp.bfloat16)
    count = tokens.shape[0]
    gathered = lax.all_gather(weight_b, "req", axis=0, tiled=True)
    regrouped = lax.all_to_all(gathered, "tp", split_axis=1, concat_axis=0, tiled=True)
    shard_rows = weight_b.shape[0]
    reordered = (
        normed.reshape(count, req_count, tp_count, shard_rows)
        .transpose(0, 2, 1, 3)
        .reshape(count, -1)
    )
    joined = jnp.dot(reordered, regrouped, preferred_element_type=jnp.float32)
    return joined + bias_block[None, :]


def shards(small, tokens, norm_gain, qkv_weight, qkv_bias, lengths):
    form = project if small else project_plain
    return attend(form(tokens, norm_gain, qkv_weight, qkv_bias), lengths)


def solution(mesh):
    placed = (
        P("req", None),
        P(("req", "tp")),
        P(("req", "tp"), None),
        P(("req", "tp")),
        P("req", None),
    )
    small = mesh.shape["req"] == 8 and mesh.shape["tp"] == 4
    return jax.shard_map(
        functools.partial(shards, small),
        mesh=mesh, in_specs=placed, out_specs=P("req", "tp"), check_vma=False,
    )
```

```python
import functools
import math

import jax
import jax.numpy as jnp
from jax import lax
from jax.experimental import pallas as pl
from jax.experimental.pallas import tpu as pltpu
from jax.sharding import PartitionSpec as P

HEAD_DIM = 128
SINKS = 4
GROUP = 7
WINDOW = 160
MOST = 256
MESH = pl.DeviceIdType.MESH


def normalize(values, gain):
    wide = values.astype(jnp.float32)
    meansq = jnp.mean(wide * wide, axis=-1, keepdims=True)
    return (wide * lax.rsqrt(meansq + 1e-06) * gain.astype(jnp.float32)).astype(jnp.bfloat16)


def starts(lens, count):
    index = jnp.arange(count, dtype=jnp.int32)
    after = index[:, None] >= jnp.cumsum(lens)[None, :]
    return jnp.sum(jnp.where(after, lens[None, :], 0), axis=1)


def rotated(v, cosine, sine):
    return (v * cosine + pltpu.roll(v, HEAD_DIM // 2, 1) * sine).astype(jnp.bfloat16)


def start_of(query_at, lens_ref):
    start, end = jnp.zeros_like(query_at), jnp.int32(0)
    for t in range(lens_ref.shape[1]):
        end = end + lens_ref[0, t]
        start = jnp.where(query_at >= end, end, start)
    return start


def attend_kernel(lens_ref, qkv_ref, out_ref):
    count = qkv_ref.shape[0]
    block = 128
    back = -(-(MOST - 1) // block)
    for at in range(count // block):
        first = max(0, at - back)
        wide = (at + 1 - first) * block
        rows = slice(at * block, (at + 1) * block)
        seen = slice(first * block, (at + 1) * block)
        query_at = at * block + lax.broadcasted_iota(jnp.int32, (block, 1), 0)
        key_at = first * block + lax.broadcasted_iota(jnp.int32, (block, wide), 1)
        start = start_of(query_at, lens_ref)
        low = jnp.maximum(query_at - (WINDOW - 1), start)
        allowed = jnp.logical_and(
            key_at <= query_at,
            jnp.logical_or(
                key_at >= low, jnp.logical_and(key_at >= start, key_at < start + SINKS)
            ),
        )
        query = jnp.concatenate(
            [qkv_ref[rows, h * HEAD_DIM : (h + 1) * HEAD_DIM] for h in range(GROUP)], axis=0
        )
        scores = lax.dot_general(
            query, qkv_ref[seen, GROUP * HEAD_DIM : (GROUP + 1) * HEAD_DIM],
            (((1,), (1,)), ((), ())), preferred_element_type=jnp.float32,
        ) * (1.0 / math.sqrt(HEAD_DIM))
        scores = jnp.where(allowed[None], scores.reshape(GROUP, block, wide), -1e30)
        peak = jnp.max(scores, axis=-1, keepdims=True)
        expo = jnp.exp(scores - peak)
        weights = (expo * (1.0 / jnp.sum(expo, axis=-1, keepdims=True))).astype(jnp.bfloat16)
        mixed = jnp.dot(
            weights.reshape(GROUP * block, wide), qkv_ref[seen, (GROUP + 1) * HEAD_DIM :],
            preferred_element_type=jnp.float32,
        ).astype(jnp.bfloat16)
        for h in range(GROUP):
            out_ref[rows, h * HEAD_DIM : (h + 1) * HEAD_DIM] = mixed[h * block : (h + 1) * block]


def attend_turned(qkv, lens):
    count = qkv.shape[0]
    vmem = pl.BlockSpec(memory_space=pltpu.VMEM)
    return pl.pallas_call(
        attend_kernel,
        out_shape=jax.ShapeDtypeStruct((count, GROUP * HEAD_DIM), jnp.bfloat16),
        in_specs=[pl.BlockSpec(memory_space=pltpu.SMEM), vmem],
        out_specs=vmem,
        compiler_params=pltpu.CompilerParams(vmem_limit_bytes=32 << 20),
        name="attention",
    )(lens, qkv)


def project_kernel(
    cuts, lens_ref, gain_ref, bias_ref, w_hbm, tok_hbm, out_ref,
    wide_w, wb, full, tok, pieces, scale, total, cosine, sine, side, sides,
    tok_sem, w_sem, first_send, first_recv, side_send, side_recv,
    ring_send, ring_recv, trail_send, trail_recv,
):
    req, tp = lax.axis_index("req"), lax.axis_index("tp")
    count, depth = tok.shape
    shard = wb.shape[1]
    width = full.shape[2]
    z, x = req // 2, req % 2
    y, core = tp // 2, tp % 2
    place = (1 - x) * z + x * (7 - z)

    def req_at(pos):
        pos = pos % 8
        far = pos // 4
        return (1 - far) * (2 * pos) + far * (2 * (7 - pos) + 1)

    right, left = req_at(place + 1), req_at(place + 7)
    peers = (2 * y + 1 - core, 2 * (1 - y) + core, 2 * (1 - y) + 1 - core)
    own = 4 * req + tp

    barrier = pltpu.get_barrier_semaphore()
    for peer in peers:
        pl.semaphore_signal(barrier, inc=1, device_id=(req, peer), device_id_type=MESH)
    for near in (left, right):
        pl.semaphore_signal(barrier, inc=1, device_id=(near, tp), device_id_type=MESH)

    loads = []
    for k, t in enumerate(peers + (tp,)):
        copy = pltpu.make_async_copy(
            w_hbm.at[:, pl.ds(pl.multiple_of(t * width, 128), width)], wide_w.at[k], w_sem.at[k]
        )
        loads.append(copy)
    for k in (0, 3, 1, 2):
        loads[k].start()
    tok_copy = pltpu.make_async_copy(tok_hbm, tok, tok_sem)
    tok_copy.start()

    def rounded(v):
        return v.astype(jnp.bfloat16).astype(jnp.float32)

    side[...] = jnp.zeros_like(side)
    side[0:1, 0:shard] = rounded(gain_ref[...])
    side[1:2, :] = rounded(bias_ref[:, 0:128])
    side[2:3, 0 : width // 8 - 128] = rounded(bias_ref[:, 128:])

    pl.semaphore_wait(barrier, 5)
    side_firsts = []
    for k, peer in enumerate(peers):
        copy = pltpu.make_async_remote_copy(
            src_ref=side, dst_ref=sides.at[core, req, y],
            send_sem=side_send.at[k], recv_sem=side_recv.at[k],
            device_id=(req, peer), device_id_type=MESH,
        )
        copy.start()
        side_firsts.append(copy)
    sides[core, req, y] = side[...]
    firsts = {}
    for k in (0, 3, 1, 2):
        loads[k].wait()
        if k == 3:
            full[own, 0:shard, :] = wide_w[k].astype(jnp.bfloat16)
            continue
        wb[k] = wide_w[k].astype(jnp.bfloat16)
        copy = pltpu.make_async_remote_copy(
            src_ref=wb.at[k], dst_ref=full.at[own, pl.ds(0, shard)],
            send_sem=first_send.at[k], recv_sem=first_recv.at[k],
            device_id=(req, peers[k]), device_id_type=MESH,
        )
        copy.start()
        firsts[k] = copy

    ring = {}
    trail = {}

    def source_of(way, hop):
        return req_at(place + 8 - hop) if way == 0 else req_at(place + hop)

    def slot_of(way, hop, piece):
        row = y if piece == 0 else 1 - y
        return 4 * source_of(way, hop) + 2 * row + way

    def send(way, hop, piece, part):
        rows = full.at[slot_of(way, hop, piece), pl.ds(cuts[part], cuts[part + 1] - cuts[part])]
        copy = pltpu.make_async_remote_copy(
            src_ref=rows, dst_ref=rows,
            send_sem=ring_send.at[way, hop, piece, part],
            recv_sem=ring_recv.at[way, hop, piece, part],
            device_id=(right if way == 0 else left, tp), device_id_type=MESH,
        )
        copy.start()
        ring[way, hop, piece, part] = copy

    def send_trail(way, hop):
        block = sides.at[way, source_of(way, hop)]
        copy = pltpu.make_async_remote_copy(
            src_ref=block, dst_ref=block,
            send_sem=trail_send.at[way, hop], recv_sem=trail_recv.at[way, hop],
            device_id=(right if way == 0 else left, tp), device_id_type=MESH,
        )
        copy.start()
        trail[way, hop] = copy

    def place_pieces(quarter):
        group = depth // 4
        base = quarter * group

        @pl.loop(0, count // 64)
        def _(i):
            rows = pl.ds(pl.multiple_of(i * 64, 64), 64)
            for k in range(8):
                lo = base + shard * k
                at = lo // 128 * 128
                span = tok[rows, at : min(at + 256, depth)].astype(jnp.float32)
                size = span.shape[1]
                if lo > at:
                    span = pltpu.roll(span, size - (lo - at), 1)
                lane = lax.broadcasted_iota(jnp.int32, (64, 128), 1)
                part = jnp.where(lane < shard, span[:, 0:128], 0.0)
                pieces[8 * quarter + k, rows, :] = part.astype(jnp.bfloat16)

    def factor(slot, way):
        gain = sides[way, slot // 4, slot % 4 // 2, 0:1, :]
        return (pieces[slot].astype(jnp.float32) * scale[...] * gain).astype(jnp.bfloat16)

    def factors(hop, piece):
        return jnp.concatenate(
            [factor(slot_of(way, hop, piece), way) for way in range(2)], axis=1
        )

    def blocks(hop, piece, columns):
        return jnp.concatenate(
            [full[slot_of(way, hop, piece), :, columns] for way in range(2)], axis=0
        )

    def multiply(hop, piece, begin=False):
        lhs = factors(hop, piece)
        for n in range(3):
            part = slice(n * (width // 3), (n + 1) * (width // 3))
            product = jnp.dot(lhs, blocks(hop, piece, part), preferred_element_type=jnp.float32)
            if begin:
                total[:, part] = product
            else:
                total[:, part] += product

    due = {
        3: ((0, 1),),
        4: ((1, 0), (2, 0), (1, 1)),
        5: ((3, 0), (2, 1), (4, 0)),
        6: ((5, 0), (3, 1), (4, 1), (6, 0)),
        7: ((5, 1), (7, 0), (6, 1)),
    }
    parts = len(cuts) - 1
    for step in range(8):
        if step == 0:
            firsts[0].wait_recv()
        for part in range(parts):
            for way in range(2):
                if step >= 1:
                    ring[way, step - 1, 0, part].wait_recv()
                if step <= 6:
                    send(way, step, 0, part)
        if step == 0:
            for copy in side_firsts:
                copy.wait_recv()
        for way in range(2):
            if step >= 1:
                trail[way, step - 1].wait_recv()
            if step <= 6:
                send_trail(way, step)
        if step == 1:
            firsts[1].wait_recv()
            firsts[2].wait_recv()
        if step >= 1:
            for part in range(parts):
                for way in range(2):
                    if step >= 2:
                        ring[way, step - 2, 1, part].wait_recv()
                    send(way, step - 1, 1, part)
        if step == 0:
            @pl.loop(0, full.shape[0])
            def _(i):
                full[i, shard:, :] = jnp.zeros((full.shape[1] - shard, width), jnp.bfloat16)

            tok_copy.wait()

            @pl.loop(0, count // 32)
            def _(i):
                rows = pl.ds(pl.multiple_of(i * 32, 32), 32)
                wide = tok[rows, :].astype(jnp.float32)
                mean = jnp.sum(wide * wide, axis=-1, keepdims=True) * (1.0 / depth)
                scale[rows, :] = jnp.broadcast_to(lax.rsqrt(mean + 1e-06), (32, 128))
        elif step == 1:
            place_pieces(0)
            place_pieces(1)
        elif step == 2:
            place_pieces(2)
            place_pieces(3)
        elif step == 3:
            at = lax.broadcasted_iota(jnp.int32, (count, 1), 0)
            pos = (at - start_of(at, lens_ref)).astype(jnp.float32)
            lane = lax.broadcasted_iota(jnp.int32, (1, HEAD_DIM), 1)
            half = HEAD_DIM // 2
            freqs = jnp.exp(
                -((lane % half).astype(jnp.float32) * 2.0 / HEAD_DIM) * math.log(1000000.0)
            )
            angle = pos * freqs
            cosine[...] = jnp.cos(angle)
            sine[...] = jnp.where(lane < half, -1.0, 1.0) * jnp.sin(angle)
            multiply(0, 0, True)
        for distance, piece in due.get(step, ()):
            multiply(distance, piece)
    lines = [
        sides[(8 * tp + i) % 2, (8 * tp + i) // 4, (8 * tp + i) % 4 // 2] for i in range(8)
    ]
    bias = jnp.zeros((8, width), jnp.float32)
    for i, both in enumerate(lines):
        line = jnp.concatenate(
            [
                pltpu.roll(both, 7, 0), pltpu.roll(both, 6, 0),
                jnp.zeros((8, width - 256), jnp.float32),
            ],
            axis=1,
        )
        bias = bias + (pltpu.roll(line, width // 8 * i, 1) if i else line)
    bias = bias[0:1, :]
    lhs = factors(7, 1)
    for part in range(parts):
        for way in range(2):
            ring[way, 6, 1, part].wait_recv()
    for n in range(3):
        lo = n * (width // 3)
        part = slice(lo, lo + width // 3)
        product = jnp.dot(lhs, blocks(7, 1, part), preferred_element_type=jnp.float32)
        joined = total[:, part] + product + bias[:, part]
        for k in range(3):
            head = 3 * n + k
            v = joined[:, k * HEAD_DIM : (k + 1) * HEAD_DIM]
            out_ref[:, head * HEAD_DIM : (head + 1) * HEAD_DIM] = (
                rotated(v, cosine[...], sine[...]) if head <= GROUP else v.astype(jnp.bfloat16)
            )
    for copy in (
        list(firsts.values()) + side_firsts + list(ring.values()) + list(trail.values())
    ):
        copy.wait_send()


def project(tokens, norm_gain, qkv_weight, qkv_bias, lens):
    count, depth = tokens.shape
    shard, columns = qkv_weight.shape
    width = columns // 4
    half = shard // 32 * 16
    cuts = (0, shard - half, shard)
    parts = len(cuts) - 1
    vmem = pl.BlockSpec(memory_space=pltpu.VMEM)
    hbm = pl.BlockSpec(memory_space=pl.ANY)
    dma = pltpu.SemaphoreType.DMA
    f32, bf16 = jnp.float32, jnp.bfloat16
    return pl.pallas_call(
        functools.partial(project_kernel, cuts),
        out_shape=jax.ShapeDtypeStruct((count, width), bf16),
        in_specs=[pl.BlockSpec(memory_space=pltpu.SMEM), vmem, vmem, hbm, hbm],
        out_specs=vmem,
        scratch_shapes=[
            pltpu.VMEM((4, shard, width), f32),
            pltpu.VMEM((3, shard, width), bf16),
            pltpu.VMEM((32, 128, width), bf16),
            pltpu.VMEM((count, depth), bf16),
            pltpu.VMEM((32, count, 128), bf16),
            pltpu.VMEM((count, 128), f32),
            pltpu.VMEM((count, width), f32),
            pltpu.VMEM((count, HEAD_DIM), f32),
            pltpu.VMEM((count, HEAD_DIM), f32),
            pltpu.VMEM((8, 128), f32),
            pltpu.VMEM((2, 8, 2, 8, 128), f32),
            dma, dma((4,)),
            dma((3,)), dma((3,)), dma((3,)), dma((3,)),
            dma((2, 7, 2, parts)), dma((2, 7, 2, parts)), dma((2, 7)), dma((2, 7)),
        ],
        compiler_params=pltpu.CompilerParams(
            collective_id=0, has_side_effects=True, vmem_limit_bytes=52 << 20
        ),
        name="project",
    )(lens, norm_gain.reshape(1, shard), qkv_bias.reshape(1, -1), qkv_weight, tokens)


def turn_plain(joined, lens):
    count = joined.shape[0]
    half = HEAD_DIM // 2
    pos = jnp.arange(count, dtype=jnp.int32) - starts(lens, count)
    freqs = jnp.exp(-(jnp.arange(half, dtype=jnp.float32) * 2.0 / HEAD_DIM) * math.log(1000000.0))
    angle = pos.astype(jnp.float32)[:, None] * freqs[None, :]
    cosine = jnp.tile(jnp.cos(angle), (1, 2))[:, None, :]
    sine = jnp.tile(jnp.sin(angle), (1, 2))[:, None, :]
    heads = joined.reshape(count, GROUP + 2, HEAD_DIM)
    spun = jnp.concatenate([-heads[..., half:], heads[..., :half]], axis=-1)
    turned = (heads * cosine + spun * sine)[:, : GROUP + 1]
    both = jnp.concatenate([turned, heads[:, GROUP + 1 :]], axis=1)
    return both.reshape(count, -1).astype(jnp.bfloat16)


def project_plain(tokens, norm_gain, qkv_weight, qkv_bias):
    tp_count = lax.axis_size("tp")
    req_count = lax.axis_size("req")
    tp_place = lax.axis_index("tp")
    gain_full, bias_full = (
        lax.all_gather(norm_gain.astype(jnp.bfloat16), ("req", "tp"), axis=0, tiled=True),
        lax.all_gather(qkv_bias.astype(jnp.bfloat16), ("req", "tp"), axis=0, tiled=True),
    )
    width = bias_full.shape[0] // tp_count
    bias_block = lax.dynamic_slice_in_dim(bias_full, tp_place * width, width).astype(jnp.float32)
    normed = normalize(tokens, gain_full)
    weight_b = qkv_weight.astype(jnp.bfloat16)
    count = tokens.shape[0]
    gathered = lax.all_gather(weight_b, "req", axis=0, tiled=True)
    regrouped = lax.all_to_all(gathered, "tp", split_axis=1, concat_axis=0, tiled=True)
    shard_rows = weight_b.shape[0]
    reordered = (
        normed.reshape(count, req_count, tp_count, shard_rows)
        .transpose(0, 2, 1, 3)
        .reshape(count, -1)
    )
    joined = jnp.dot(reordered, regrouped, preferred_element_type=jnp.float32)
    return joined + bias_block[None, :]


def shards(small, tokens, norm_gain, qkv_weight, qkv_bias, lengths):
    if small:
        qkv = project(tokens, norm_gain, qkv_weight, qkv_bias, lengths)
    else:
        qkv = turn_plain(project_plain(tokens, norm_gain, qkv_weight, qkv_bias), lengths[0])
    return attend_turned(qkv, lengths)


def solution(mesh):
    placed = (
        P("req", None),
        P(("req", "tp")),
        P(("req", "tp"), None),
        P(("req", "tp")),
        P("req", None),
    )
    small = mesh.shape["req"] == 8 and mesh.shape["tp"] == 4
    return jax.shard_map(
        functools.partial(shards, small),
        mesh=mesh, in_specs=placed, out_specs=P("req", "tp"), check_vma=False,
    )
```

```python
import functools
import math

import jax
import jax.numpy as jnp
from jax import lax
from jax.experimental import pallas as pl
from jax.experimental.pallas import tpu as pltpu
from jax.sharding import PartitionSpec as P

HEAD_DIM = 128
SINKS = 4
GROUP = 7
WINDOW = 160
MOST = 256
MESH = pl.DeviceIdType.MESH


def normalize(values, gain):
    wide = values.astype(jnp.float32)
    meansq = jnp.mean(wide * wide, axis=-1, keepdims=True)
    return (wide * lax.rsqrt(meansq + 1e-06) * gain.astype(jnp.float32)).astype(jnp.bfloat16)


def starts(lens, count):
    index = jnp.arange(count, dtype=jnp.int32)
    after = index[:, None] >= jnp.cumsum(lens)[None, :]
    return jnp.sum(jnp.where(after, lens[None, :], 0), axis=1)


def rotated(v, cosine, sine):
    return (v * cosine + pltpu.roll(v, HEAD_DIM // 2, 1) * sine).astype(jnp.bfloat16)


def start_of(query_at, lens_ref):
    start, end = jnp.zeros_like(query_at), jnp.int32(0)
    for t in range(lens_ref.shape[1]):
        end = end + lens_ref[0, t]
        start = jnp.where(query_at >= end, end, start)
    return start


def attend_block(at, query, keys, values, lens_ref):
    block = 128
    first = max(0, at - -(-(MOST - 1) // block))
    wide = (at + 1 - first) * block
    heads = query.shape[0] // block
    query_at = at * block + lax.broadcasted_iota(jnp.int32, (block, 1), 0)
    key_at = first * block + lax.broadcasted_iota(jnp.int32, (block, wide), 1)
    start = start_of(query_at, lens_ref)
    low = jnp.maximum(query_at - (WINDOW - 1), start)
    allowed = jnp.logical_and(
        key_at <= query_at,
        jnp.logical_or(key_at >= low, jnp.logical_and(key_at >= start, key_at < start + SINKS)),
    )
    seen = slice(first * block, (at + 1) * block)
    scores = lax.dot_general(
        query, keys(seen), (((1,), (1,)), ((), ())), preferred_element_type=jnp.float32
    ) * (1.0 / math.sqrt(HEAD_DIM))
    scores = jnp.where(allowed[None], scores.reshape(heads, block, wide), -1e30)
    peak = jnp.max(scores, axis=-1, keepdims=True)
    expo = jnp.exp(scores - peak)
    weights = (expo * (1.0 / jnp.sum(expo, axis=-1, keepdims=True))).astype(jnp.bfloat16)
    return jnp.dot(
        weights.reshape(heads * block, wide), values(seen), preferred_element_type=jnp.float32
    ).astype(jnp.bfloat16)


def attend_heads(at, heads, shift, source, key, value, out_ref, lens_ref):
    rows = slice(at * 128, (at + 1) * 128)
    query = jnp.concatenate(
        [source[rows, h * HEAD_DIM : (h + 1) * HEAD_DIM] for h in heads], axis=0
    )
    mixed = attend_block(at, query, key, value, lens_ref)
    for i, h in enumerate(heads):
        column = (h - shift) * HEAD_DIM
        out_ref[rows, column : column + HEAD_DIM] = mixed[i * 128 : (i + 1) * 128]


def attend_kernel(heads, lens_ref, qkv_ref, *refs):
    out_ref = refs[-1]
    part = lambda c: lambda seen: qkv_ref[seen, c * HEAD_DIM : (c + 1) * HEAD_DIM]
    for at in range(qkv_ref.shape[0] // 128):
        attend_heads(
            at, range(heads), 0, qkv_ref, part(heads), part(heads + 1), out_ref, lens_ref
        )
    if len(refs) > 1:
        out_ref[:, heads * HEAD_DIM :] = refs[0][...]


def attend_turned(lens, qkv, *done):
    count = qkv.shape[0]
    vmem = pl.BlockSpec(memory_space=pltpu.VMEM)
    return pl.pallas_call(
        functools.partial(attend_kernel, qkv.shape[1] // HEAD_DIM - 2),
        out_shape=jax.ShapeDtypeStruct((count, GROUP * HEAD_DIM), jnp.bfloat16),
        in_specs=[pl.BlockSpec(memory_space=pltpu.SMEM)] + [vmem] * (1 + len(done)),
        out_specs=vmem,
        compiler_params=pltpu.CompilerParams(vmem_limit_bytes=32 << 20),
        name="attention",
    )(lens, qkv, *done)


def project_kernel(
    lens_hbm, gain_hbm, bias_hbm, w_hbm, tok_hbm, out_ref, done_ref,
    lens_ref, gain_ref, bias_ref, small_sem, turned, line_ref, wide_w, wb, full, tok, pieces, scale, total, cosine, sine, side, sides,
    tok_sem, w_sem, first_send, first_recv, side_send, side_recv,
    ring_send, ring_recv, trail_send, trail_recv,
):
    req, tp = lax.axis_index("req"), lax.axis_index("tp")
    count, depth = tok.shape
    shard = wb.shape[1]
    width = full.shape[2]
    z, x = req // 2, req % 2
    y, core = tp // 2, tp % 2
    place = (1 - x) * z + x * (7 - z)

    def req_at(pos):
        pos = pos % 8
        far = pos // 4
        return (1 - far) * (2 * pos) + far * (2 * (7 - pos) + 1)

    right, left = req_at(place + 1), req_at(place + 7)
    peers = (2 * y + 1 - core, 2 * (1 - y) + core, 2 * (1 - y) + 1 - core)
    own = 4 * req + tp

    barrier = pltpu.get_barrier_semaphore()
    for peer in peers:
        pl.semaphore_signal(barrier, inc=1, device_id=(req, peer), device_id_type=MESH)
    for near in (left, right):
        pl.semaphore_signal(barrier, inc=1, device_id=(near, tp), device_id_type=MESH)

    smalls = [
        pltpu.make_async_copy(source, to, small_sem.at[k])
        for k, (source, to) in enumerate(
            ((gain_hbm, gain_ref), (bias_hbm, bias_ref), (lens_hbm, lens_ref))
        )
    ]
    for copy in smalls:
        copy.start()
    loads = []
    for k, t in enumerate(peers + (tp,)):
        copy = pltpu.make_async_copy(
            w_hbm.at[:, pl.ds(pl.multiple_of(t * width, 128), width)], wide_w.at[k], w_sem.at[k]
        )
        loads.append(copy)
    for k in (0, 3, 1, 2):
        loads[k].start()
    tok_copy = pltpu.make_async_copy(tok_hbm, tok, tok_sem)
    tok_copy.start()

    def rounded(v):
        return v.astype(jnp.bfloat16).astype(jnp.float32)

    for copy in smalls:
        copy.wait()
    side[...] = jnp.zeros_like(side)
    side[0:1, 0:shard] = rounded(gain_ref[...])
    side[1:2, :] = rounded(bias_ref[:, 0:128])
    side[2:3, 0 : width // 8 - 128] = rounded(bias_ref[:, 128:])

    pl.semaphore_wait(barrier, 5)
    side_firsts = []
    for k, peer in enumerate(peers):
        copy = pltpu.make_async_remote_copy(
            src_ref=side, dst_ref=sides.at[core, req, y],
            send_sem=side_send.at[k], recv_sem=side_recv.at[k],
            device_id=(req, peer), device_id_type=MESH,
        )
        copy.start()
        side_firsts.append(copy)
    sides[core, req, y] = side[...]
    firsts = {}
    for k in (0, 3, 1, 2):
        loads[k].wait()
        if k == 3:
            full[own, 0:shard, :] = wide_w[k].astype(jnp.bfloat16)
            continue
        wb[k] = wide_w[k].astype(jnp.bfloat16)
        copy = pltpu.make_async_remote_copy(
            src_ref=wb.at[k], dst_ref=full.at[own, pl.ds(0, shard)],
            send_sem=first_send.at[k], recv_sem=first_recv.at[k],
            device_id=(req, peers[k]), device_id_type=MESH,
        )
        copy.start()
        firsts[k] = copy

    ring = {}
    trail = {}

    def source_of(way, hop):
        return req_at(place + 8 - hop) if way == 0 else req_at(place + hop)

    def slot_of(way, hop, piece):
        row = y if piece == 0 else 1 - y
        return 4 * source_of(way, hop) + 2 * row + way

    phases = ((5, 9), (2, 5), (0, 2))

    def send(way, turn, piece):
        lo, hi = phases[turn // 7]
        block = full.at[
            slot_of(way, turn % 7, piece),
            pl.ds(0, shard),
            pl.ds(lo * HEAD_DIM, (hi - lo) * HEAD_DIM),
        ]
        copy = pltpu.make_async_remote_copy(
            src_ref=block, dst_ref=block,
            send_sem=ring_send.at[way, turn, piece], recv_sem=ring_recv.at[way, turn, piece],
            device_id=(right if way == 0 else left, tp), device_id_type=MESH,
        )
        copy.start()
        ring[way, turn, piece] = copy

    def pass_on(turn, piece):
        for way in range(2):
            if turn <= 20 and turn % 7 == 0:
                send(way, turn, piece)
            if turn >= 1:
                ring[way, turn - 1, piece].wait_recv()
            if turn <= 20 and turn % 7:
                send(way, turn, piece)

    def send_trail(way, hop):
        block = sides.at[way, source_of(way, hop)]
        copy = pltpu.make_async_remote_copy(
            src_ref=block, dst_ref=block,
            send_sem=trail_send.at[way, hop], recv_sem=trail_recv.at[way, hop],
            device_id=(right if way == 0 else left, tp), device_id_type=MESH,
        )
        copy.start()
        trail[way, hop] = copy

    def place_pieces(quarter):
        group = depth // 4
        base = quarter * group

        @pl.loop(0, count // 64)
        def _(i):
            rows = pl.ds(pl.multiple_of(i * 64, 64), 64)
            for k in range(8):
                lo = base + shard * k
                at = lo // 128 * 128
                span = tok[rows, at : min(at + 256, depth)].astype(jnp.float32)
                size = span.shape[1]
                if lo > at:
                    span = pltpu.roll(span, size - (lo - at), 1)
                lane = lax.broadcasted_iota(jnp.int32, (64, 128), 1)
                part = jnp.where(lane < shard, span[:, 0:128], 0.0)
                pieces[8 * quarter + k, rows, :] = part.astype(jnp.bfloat16)

    def factor(slot, way):
        gain = sides[way, slot // 4, slot % 4 // 2, 0:1, :]
        return (pieces[slot].astype(jnp.float32) * scale[...] * gain).astype(jnp.bfloat16)

    def factors(hop, piece):
        return jnp.concatenate(
            [factor(slot_of(way, hop, piece), way) for way in range(2)], axis=1
        )

    def product(lhs, phase, distance, piece):
        lo, hi = phases[phase]
        columns = slice(lo * HEAD_DIM, hi * HEAD_DIM)
        rhs = jnp.concatenate(
            [full[slot_of(way, distance, piece), :, columns] for way in range(2)], axis=0
        )
        return columns, jnp.dot(lhs, rhs, preferred_element_type=jnp.float32)

    def multiply(phase, distance, piece):
        columns, term = product(factors(distance, piece), phase, distance, piece)
        if distance == 0 and piece == 0:
            total[:, columns] = term
        else:
            total[:, columns] += term

    def turn_head(head, joined):
        column = slice(head * HEAD_DIM, (head + 1) * HEAD_DIM)
        v = joined + line_ref[0:1, column]
        return rotated(v, cosine[...], sine[...]) if head <= GROUP else v.astype(jnp.bfloat16)

    def finish(phase):
        for head in range(*phases[phase]):
            column = slice(head * HEAD_DIM, (head + 1) * HEAD_DIM)
            turned[:, column] = turn_head(head, total[:, column])

    def part_of(c):
        return lambda seen: turned[seen, c * HEAD_DIM : (c + 1) * HEAD_DIM]

    def heads_of(at, heads):
        attend_heads(
            at, heads, 2, turned, part_of(GROUP), part_of(GROUP + 1), done_ref, lens_ref
        )

    def make_bias():
        bias = jnp.zeros((8, width), jnp.float32)
        for i in range(8):
            owner = 8 * tp + i
            both = sides[owner % 2, owner // 4, owner % 4 // 2]
            line = jnp.concatenate(
                [
                    pltpu.roll(both, 7, 0), pltpu.roll(both, 6, 0),
                    jnp.zeros((8, width - 256), jnp.float32),
                ],
                axis=1,
            )
            bias = bias + (pltpu.roll(line, width // 8 * i, 1) if i else line)
        line_ref[...] = bias

    due = {step: [] for step in range(22)}
    for d in range(8):
        for piece in range(2):
            due[max(6 + d // 3, d + piece)].append((0, d, piece))
            due[max(9 + d * 3 // 4, 7 + d + piece)].append((1, d, piece))
            if (d, piece) != (7, 1):
                due[max(16, 14 + d + piece)].append((2, d, piece))

    for step in range(22):
        if step == 0:
            firsts[0].wait_recv()
        pass_on(step, 0)
        if step == 0:
            for copy in side_firsts:
                copy.wait_recv()
        if step <= 7:
            for way in range(2):
                if step >= 1:
                    trail[way, step - 1].wait_recv()
                if step <= 6:
                    send_trail(way, step)
        if step == 1:
            firsts[1].wait_recv()
            firsts[2].wait_recv()
        if step >= 1:
            pass_on(step - 1, 1)
        if step == 0:
            @pl.loop(0, full.shape[0])
            def _(i):
                full[i, shard:, :] = jnp.zeros((full.shape[1] - shard, width), jnp.bfloat16)

            tok_copy.wait()

            @pl.loop(0, count // 32)
            def _(i):
                rows = pl.ds(pl.multiple_of(i * 32, 32), 32)
                wide = tok[rows, :].astype(jnp.float32)
                mean = jnp.sum(wide * wide, axis=-1, keepdims=True) * (1.0 / depth)
                scale[rows, :] = jnp.broadcast_to(lax.rsqrt(mean + 1e-06), (32, 128))
        elif step <= 4:
            place_pieces(step - 1)
        elif step == 5:
            at = lax.broadcasted_iota(jnp.int32, (count, 1), 0)
            pos = (at - start_of(at, lens_ref)).astype(jnp.float32)
            lane = lax.broadcasted_iota(jnp.int32, (1, HEAD_DIM), 1)
            half = HEAD_DIM // 2
            freqs = jnp.exp(
                -((lane % half).astype(jnp.float32) * 2.0 / HEAD_DIM) * math.log(1000000.0)
            )
            angle = pos * freqs
            cosine[...] = jnp.cos(angle)
            sine[...] = jnp.where(lane < half, -1.0, 1.0) * jnp.sin(angle)
        for item in due[step]:
            multiply(*item)
        if step == 8:
            make_bias()
            finish(0)
        if 9 <= step <= 12:
            heads_of(step - 9, (5, 6))
        if step == 15:
            finish(1)
        if 16 <= step <= 19:
            heads_of(step - 16, (2, 3, 4))
    out_ref[:, 2 * HEAD_DIM :] = turned[:, GROUP * HEAD_DIM :]
    lhs = factors(7, 1)
    for way in range(2):
        ring[way, 20, 1].wait_recv()
    columns, term = product(lhs, 2, 7, 1)
    joined = total[:, columns] + term
    for head in range(2):
        column = slice(head * HEAD_DIM, (head + 1) * HEAD_DIM)
        out_ref[:, column] = turn_head(head, joined[:, column])
    for copy in (
        list(firsts.values()) + side_firsts + list(ring.values()) + list(trail.values())
    ):
        copy.wait_send()


def project(tokens, norm_gain, qkv_weight, qkv_bias, lens):
    count, depth = tokens.shape
    shard, columns = qkv_weight.shape
    width = columns // 4
    vmem = pl.BlockSpec(memory_space=pltpu.VMEM)
    hbm = pl.BlockSpec(memory_space=pltpu.HBM)
    dma = pltpu.SemaphoreType.DMA
    f32, bf16 = jnp.float32, jnp.bfloat16
    return pl.pallas_call(
        project_kernel,
        out_shape=(
            jax.ShapeDtypeStruct((count, 4 * HEAD_DIM), bf16),
            jax.ShapeDtypeStruct((count, (GROUP - 2) * HEAD_DIM), bf16),
        ),
        in_specs=[hbm] * 5,
        out_specs=(vmem, vmem),
        scratch_shapes=[
            pltpu.SMEM(lens.shape, jnp.int32),
            pltpu.VMEM((1, shard), f32),
            pltpu.VMEM((1, columns // 32), f32),
            dma((3,)),
            pltpu.VMEM((count, width), bf16),
            pltpu.VMEM((8, width), f32),
            pltpu.VMEM((4, shard, width), f32),
            pltpu.VMEM((3, shard, width), bf16),
            pltpu.VMEM((32, 128, width), bf16),
            pltpu.VMEM((count, depth), bf16),
            pltpu.VMEM((32, count, 128), bf16),
            pltpu.VMEM((count, 128), f32),
            pltpu.VMEM((count, width), f32),
            pltpu.VMEM((count, HEAD_DIM), f32),
            pltpu.VMEM((count, HEAD_DIM), f32),
            pltpu.VMEM((8, 128), f32),
            pltpu.VMEM((2, 8, 2, 8, 128), f32),
            dma, dma((4,)),
            dma((3,)), dma((3,)), dma((3,)), dma((3,)),
            dma((2, 21, 2)), dma((2, 21, 2)), dma((2, 7)), dma((2, 7)),
        ],
        compiler_params=pltpu.CompilerParams(
            collective_id=0, has_side_effects=True, vmem_limit_bytes=52 << 20
        ),
        name="project",
    )(lens, norm_gain.reshape(1, shard), qkv_bias.reshape(1, -1), qkv_weight, tokens)


def turn_plain(joined, lens):
    count = joined.shape[0]
    half = HEAD_DIM // 2
    pos = jnp.arange(count, dtype=jnp.int32) - starts(lens, count)
    freqs = jnp.exp(-(jnp.arange(half, dtype=jnp.float32) * 2.0 / HEAD_DIM) * math.log(1000000.0))
    angle = pos.astype(jnp.float32)[:, None] * freqs[None, :]
    cosine = jnp.tile(jnp.cos(angle), (1, 2))[:, None, :]
    sine = jnp.tile(jnp.sin(angle), (1, 2))[:, None, :]
    heads = joined.reshape(count, GROUP + 2, HEAD_DIM)
    spun = jnp.concatenate([-heads[..., half:], heads[..., :half]], axis=-1)
    turned = (heads * cosine + spun * sine)[:, : GROUP + 1]
    both = jnp.concatenate([turned, heads[:, GROUP + 1 :]], axis=1)
    return both.reshape(count, -1).astype(jnp.bfloat16)


def project_plain(tokens, norm_gain, qkv_weight, qkv_bias):
    tp_count = lax.axis_size("tp")
    req_count = lax.axis_size("req")
    tp_place = lax.axis_index("tp")
    gain_full, bias_full = (
        lax.all_gather(norm_gain.astype(jnp.bfloat16), ("req", "tp"), axis=0, tiled=True),
        lax.all_gather(qkv_bias.astype(jnp.bfloat16), ("req", "tp"), axis=0, tiled=True),
    )
    width = bias_full.shape[0] // tp_count
    bias_block = lax.dynamic_slice_in_dim(bias_full, tp_place * width, width).astype(jnp.float32)
    normed = normalize(tokens, gain_full)
    weight_b = qkv_weight.astype(jnp.bfloat16)
    count = tokens.shape[0]
    gathered = lax.all_gather(weight_b, "req", axis=0, tiled=True)
    regrouped = lax.all_to_all(gathered, "tp", split_axis=1, concat_axis=0, tiled=True)
    shard_rows = weight_b.shape[0]
    reordered = (
        normed.reshape(count, req_count, tp_count, shard_rows)
        .transpose(0, 2, 1, 3)
        .reshape(count, -1)
    )
    joined = jnp.dot(reordered, regrouped, preferred_element_type=jnp.float32)
    return joined + bias_block[None, :]


def shards(small, tokens, norm_gain, qkv_weight, qkv_bias, lengths):
    if small:
        return attend_turned(
            lengths, *project(tokens, norm_gain, qkv_weight, qkv_bias, lengths)
        )
    qkv = turn_plain(project_plain(tokens, norm_gain, qkv_weight, qkv_bias), lengths[0])
    return attend_turned(lengths, qkv)


def solution(mesh):
    placed = (
        P("req", None),
        P(("req", "tp")),
        P(("req", "tp"), None),
        P(("req", "tp")),
        P("req", None),
    )
    small = mesh.shape["req"] == 8 and mesh.shape["tp"] == 4
    return jax.shard_map(
        functools.partial(shards, small),
        mesh=mesh, in_specs=placed, out_specs=P("req", "tp"), check_vma=False,
    )
```

```python
import functools
import math

import jax
import jax.numpy as jnp
from jax import lax
from jax.experimental import pallas as pl
from jax.experimental.pallas import tpu as pltpu
from jax.sharding import PartitionSpec as P

HEAD_DIM = 128
SINKS = 4
GROUP = 7
WINDOW = 160
MOST = 256
MESH = pl.DeviceIdType.MESH


def normalize(values, gain):
    wide = values.astype(jnp.float32)
    meansq = jnp.mean(wide * wide, axis=-1, keepdims=True)
    return (wide * lax.rsqrt(meansq + 1e-06) * gain.astype(jnp.float32)).astype(jnp.bfloat16)


def starts(lens, count):
    index = jnp.arange(count, dtype=jnp.int32)
    after = index[:, None] >= jnp.cumsum(lens)[None, :]
    return jnp.sum(jnp.where(after, lens[None, :], 0), axis=1)


def rotated(v, cosine, sine):
    return (v * cosine + pltpu.roll(v, HEAD_DIM // 2, 1) * sine).astype(jnp.bfloat16)


def start_of(query_at, lens_ref):
    start, end = jnp.zeros_like(query_at), jnp.int32(0)
    for t in range(lens_ref.shape[1]):
        end = end + lens_ref[0, t]
        start = jnp.where(query_at >= end, end, start)
    return start


def attend_kernel(lens_ref, qkv_ref, out_ref):
    count = qkv_ref.shape[0]
    block = 128
    back = -(-(MOST - 1) // block)
    for at in range(count // block):
        first = max(0, at - back)
        wide = (at + 1 - first) * block
        rows = slice(at * block, (at + 1) * block)
        seen = slice(first * block, (at + 1) * block)
        query_at = at * block + lax.broadcasted_iota(jnp.int32, (block, 1), 0)
        key_at = first * block + lax.broadcasted_iota(jnp.int32, (block, wide), 1)
        start = start_of(query_at, lens_ref)
        low = jnp.maximum(query_at - (WINDOW - 1), start)
        allowed = jnp.logical_and(
            key_at <= query_at,
            jnp.logical_or(
                key_at >= low, jnp.logical_and(key_at >= start, key_at < start + SINKS)
            ),
        )
        query = jnp.concatenate(
            [qkv_ref[rows, h * HEAD_DIM : (h + 1) * HEAD_DIM] for h in range(GROUP)], axis=0
        )
        scores = lax.dot_general(
            query, qkv_ref[seen, GROUP * HEAD_DIM : (GROUP + 1) * HEAD_DIM],
            (((1,), (1,)), ((), ())), preferred_element_type=jnp.float32,
        ) * (1.0 / math.sqrt(HEAD_DIM))
        scores = jnp.where(allowed[None], scores.reshape(GROUP, block, wide), -1e30)
        peak = jnp.max(scores, axis=-1, keepdims=True)
        expo = jnp.exp(scores - peak)
        weights = (expo * (1.0 / jnp.sum(expo, axis=-1, keepdims=True))).astype(jnp.bfloat16)
        mixed = jnp.dot(
            weights.reshape(GROUP * block, wide), qkv_ref[seen, (GROUP + 1) * HEAD_DIM :],
            preferred_element_type=jnp.float32,
        ).astype(jnp.bfloat16)
        for h in range(GROUP):
            out_ref[rows, h * HEAD_DIM : (h + 1) * HEAD_DIM] = mixed[h * block : (h + 1) * block]


def attend_turned(qkv, lens):
    count = qkv.shape[0]
    vmem = pl.BlockSpec(memory_space=pltpu.VMEM)
    return pl.pallas_call(
        attend_kernel,
        out_shape=jax.ShapeDtypeStruct((count, GROUP * HEAD_DIM), jnp.bfloat16),
        in_specs=[pl.BlockSpec(memory_space=pltpu.SMEM), vmem],
        out_specs=vmem,
        compiler_params=pltpu.CompilerParams(vmem_limit_bytes=32 << 20),
        name="attention",
    )(lens, qkv)


def project_kernel(
    cuts, lens_hbm, gain_hbm, bias_hbm, w_hbm, tok_hbm, out_ref,
    lens_ref, gain_ref, bias_ref, small_sem, wide_w, wb, full, tok, pieces, scale, total, cosine, sine, side, sides,
    tok_sem, w_sem, first_send, first_recv, side_send, side_recv,
    ring_send, ring_recv, trail_send, trail_recv,
):
    req, tp = lax.axis_index("req"), lax.axis_index("tp")
    count, depth = tok.shape
    shard = wb.shape[1]
    width = full.shape[2]
    z, x = req // 2, req % 2
    y, core = tp // 2, tp % 2
    place = (1 - x) * z + x * (7 - z)

    def req_at(pos):
        pos = pos % 8
        far = pos // 4
        return (1 - far) * (2 * pos) + far * (2 * (7 - pos) + 1)

    right, left = req_at(place + 1), req_at(place + 7)
    peers = (2 * y + 1 - core, 2 * (1 - y) + core, 2 * (1 - y) + 1 - core)
    own = 4 * req + tp

    barrier = pltpu.get_barrier_semaphore()
    for peer in peers:
        pl.semaphore_signal(barrier, inc=1, device_id=(req, peer), device_id_type=MESH)
    for near in (left, right):
        pl.semaphore_signal(barrier, inc=1, device_id=(near, tp), device_id_type=MESH)

    smalls = [
        pltpu.make_async_copy(source, to, small_sem.at[k])
        for k, (source, to) in enumerate(
            ((gain_hbm, gain_ref), (bias_hbm, bias_ref), (lens_hbm, lens_ref))
        )
    ]
    for copy in smalls:
        copy.start()
    loads = []
    for k, t in enumerate(peers + (tp,)):
        copy = pltpu.make_async_copy(
            w_hbm.at[:, pl.ds(pl.multiple_of(t * width, 128), width)], wide_w.at[k], w_sem.at[k]
        )
        loads.append(copy)
    for k in (0, 3, 1, 2):
        loads[k].start()
    tok_copy = pltpu.make_async_copy(tok_hbm, tok, tok_sem)
    tok_copy.start()

    def rounded(v):
        return v.astype(jnp.bfloat16).astype(jnp.float32)

    for copy in smalls:
        copy.wait()
    side[...] = jnp.zeros_like(side)
    side[0:1, 0:shard] = rounded(gain_ref[...])
    side[1:2, :] = rounded(bias_ref[:, 0:128])
    side[2:3, 0 : width // 8 - 128] = rounded(bias_ref[:, 128:])

    pl.semaphore_wait(barrier, 5)
    side_firsts = []
    for k, peer in enumerate(peers):
        copy = pltpu.make_async_remote_copy(
            src_ref=side, dst_ref=sides.at[core, req, y],
            send_sem=side_send.at[k], recv_sem=side_recv.at[k],
            device_id=(req, peer), device_id_type=MESH,
        )
        copy.start()
        side_firsts.append(copy)
    sides[core, req, y] = side[...]
    firsts = {}
    for k in (0, 3, 1, 2):
        loads[k].wait()
        if k == 3:
            full[own, 0:shard, :] = wide_w[k].astype(jnp.bfloat16)
            continue
        wb[k] = wide_w[k].astype(jnp.bfloat16)
        copy = pltpu.make_async_remote_copy(
            src_ref=wb.at[k], dst_ref=full.at[own, pl.ds(0, shard)],
            send_sem=first_send.at[k], recv_sem=first_recv.at[k],
            device_id=(req, peers[k]), device_id_type=MESH,
        )
        copy.start()
        firsts[k] = copy

    ring = {}
    trail = {}

    def source_of(way, hop):
        return req_at(place + 8 - hop) if way == 0 else req_at(place + hop)

    def slot_of(way, hop, piece):
        row = y if piece == 0 else 1 - y
        return 4 * source_of(way, hop) + 2 * row + way

    def send(way, hop, piece, part):
        rows = full.at[slot_of(way, hop, piece), pl.ds(cuts[part], cuts[part + 1] - cuts[part])]
        copy = pltpu.make_async_remote_copy(
            src_ref=rows, dst_ref=rows,
            send_sem=ring_send.at[way, hop, piece, part],
            recv_sem=ring_recv.at[way, hop, piece, part],
            device_id=(right if way == 0 else left, tp), device_id_type=MESH,
        )
        copy.start()
        ring[way, hop, piece, part] = copy

    def send_trail(way, hop):
        block = sides.at[way, source_of(way, hop)]
        copy = pltpu.make_async_remote_copy(
            src_ref=block, dst_ref=block,
            send_sem=trail_send.at[way, hop], recv_sem=trail_recv.at[way, hop],
            device_id=(right if way == 0 else left, tp), device_id_type=MESH,
        )
        copy.start()
        trail[way, hop] = copy

    def place_pieces(quarter):
        group = depth // 4
        base = quarter * group

        @pl.loop(0, count // 64)
        def _(i):
            rows = pl.ds(pl.multiple_of(i * 64, 64), 64)
            for k in range(8):
                lo = base + shard * k
                at = lo // 128 * 128
                span = tok[rows, at : min(at + 256, depth)].astype(jnp.float32)
                size = span.shape[1]
                if lo > at:
                    span = pltpu.roll(span, size - (lo - at), 1)
                lane = lax.broadcasted_iota(jnp.int32, (64, 128), 1)
                part = jnp.where(lane < shard, span[:, 0:128], 0.0)
                pieces[8 * quarter + k, rows, :] = part.astype(jnp.bfloat16)

    def factor(slot, way):
        gain = sides[way, slot // 4, slot % 4 // 2, 0:1, :]
        return (pieces[slot].astype(jnp.float32) * scale[...] * gain).astype(jnp.bfloat16)

    def factors(hop, piece):
        return jnp.concatenate(
            [factor(slot_of(way, hop, piece), way) for way in range(2)], axis=1
        )

    def blocks(hop, piece, columns):
        return jnp.concatenate(
            [full[slot_of(way, hop, piece), :, columns] for way in range(2)], axis=0
        )

    def multiply(hop, piece, begin=False):
        lhs = factors(hop, piece)
        for n in range(3):
            part = slice(n * (width // 3), (n + 1) * (width // 3))
            product = jnp.dot(lhs, blocks(hop, piece, part), preferred_element_type=jnp.float32)
            if begin:
                total[:, part] = product
            else:
                total[:, part] += product

    due = {
        3: ((0, 1),),
        4: ((1, 0), (2, 0), (1, 1)),
        5: ((3, 0), (2, 1), (4, 0)),
        6: ((5, 0), (3, 1), (4, 1), (6, 0)),
        7: ((5, 1), (7, 0), (6, 1)),
    }
    parts = len(cuts) - 1
    for step in range(8):
        if step == 0:
            firsts[0].wait_recv()
        for part in range(parts):
            for way in range(2):
                if step >= 1:
                    ring[way, step - 1, 0, part].wait_recv()
                if step <= 6:
                    send(way, step, 0, part)
        if step == 0:
            for copy in side_firsts:
                copy.wait_recv()
        for way in range(2):
            if step >= 1:
                trail[way, step - 1].wait_recv()
            if step <= 6:
                send_trail(way, step)
        if step == 1:
            firsts[1].wait_recv()
            firsts[2].wait_recv()
        if step >= 1:
            for part in range(parts):
                for way in range(2):
                    if step >= 2:
                        ring[way, step - 2, 1, part].wait_recv()
                    send(way, step - 1, 1, part)
        if step == 0:
            @pl.loop(0, full.shape[0])
            def _(i):
                full[i, shard:, :] = jnp.zeros((full.shape[1] - shard, width), jnp.bfloat16)

            tok_copy.wait()

            @pl.loop(0, count // 32)
            def _(i):
                rows = pl.ds(pl.multiple_of(i * 32, 32), 32)
                wide = tok[rows, :].astype(jnp.float32)
                mean = jnp.sum(wide * wide, axis=-1, keepdims=True) * (1.0 / depth)
                scale[rows, :] = jnp.broadcast_to(lax.rsqrt(mean + 1e-06), (32, 128))
        elif step == 1:
            place_pieces(0)
            place_pieces(1)
        elif step == 2:
            place_pieces(2)
            place_pieces(3)
        elif step == 3:
            at = lax.broadcasted_iota(jnp.int32, (count, 1), 0)
            pos = (at - start_of(at, lens_ref)).astype(jnp.float32)
            lane = lax.broadcasted_iota(jnp.int32, (1, HEAD_DIM), 1)
            half = HEAD_DIM // 2
            freqs = jnp.exp(
                -((lane % half).astype(jnp.float32) * 2.0 / HEAD_DIM) * math.log(1000000.0)
            )
            angle = pos * freqs
            cosine[...] = jnp.cos(angle)
            sine[...] = jnp.where(lane < half, -1.0, 1.0) * jnp.sin(angle)
            multiply(0, 0, True)
        for distance, piece in due.get(step, ()):
            multiply(distance, piece)
    lines = [
        sides[(8 * tp + i) % 2, (8 * tp + i) // 4, (8 * tp + i) % 4 // 2] for i in range(8)
    ]
    bias = jnp.zeros((8, width), jnp.float32)
    for i, both in enumerate(lines):
        line = jnp.concatenate(
            [
                pltpu.roll(both, 7, 0), pltpu.roll(both, 6, 0),
                jnp.zeros((8, width - 256), jnp.float32),
            ],
            axis=1,
        )
        bias = bias + (pltpu.roll(line, width // 8 * i, 1) if i else line)
    bias = bias[0:1, :]
    lhs = factors(7, 1)
    for part in range(parts):
        for way in range(2):
            ring[way, 6, 1, part].wait_recv()
    for n in range(3):
        lo = n * (width // 3)
        part = slice(lo, lo + width // 3)
        product = jnp.dot(lhs, blocks(7, 1, part), preferred_element_type=jnp.float32)
        joined = total[:, part] + product + bias[:, part]
        for k in range(3):
            head = 3 * n + k
            v = joined[:, k * HEAD_DIM : (k + 1) * HEAD_DIM]
            out_ref[:, head * HEAD_DIM : (head + 1) * HEAD_DIM] = (
                rotated(v, cosine[...], sine[...]) if head <= GROUP else v.astype(jnp.bfloat16)
            )
    for copy in (
        list(firsts.values()) + side_firsts + list(ring.values()) + list(trail.values())
    ):
        copy.wait_send()


def project(tokens, norm_gain, qkv_weight, qkv_bias, lens):
    count, depth = tokens.shape
    shard, columns = qkv_weight.shape
    width = columns // 4
    half = shard // 32 * 16
    cuts = (0, shard - half, shard)
    parts = len(cuts) - 1
    vmem = pl.BlockSpec(memory_space=pltpu.VMEM)
    hbm = pl.BlockSpec(memory_space=pltpu.HBM)
    dma = pltpu.SemaphoreType.DMA
    f32, bf16 = jnp.float32, jnp.bfloat16
    return pl.pallas_call(
        functools.partial(project_kernel, cuts),
        out_shape=jax.ShapeDtypeStruct((count, width), bf16),
        in_specs=[hbm] * 5,
        out_specs=vmem,
        scratch_shapes=[
            pltpu.SMEM(lens.shape, jnp.int32),
            pltpu.VMEM((1, shard), f32),
            pltpu.VMEM((1, columns // 32), f32),
            dma((3,)),
            pltpu.VMEM((4, shard, width), f32),
            pltpu.VMEM((3, shard, width), bf16),
            pltpu.VMEM((32, 128, width), bf16),
            pltpu.VMEM((count, depth), bf16),
            pltpu.VMEM((32, count, 128), bf16),
            pltpu.VMEM((count, 128), f32),
            pltpu.VMEM((count, width), f32),
            pltpu.VMEM((count, HEAD_DIM), f32),
            pltpu.VMEM((count, HEAD_DIM), f32),
            pltpu.VMEM((8, 128), f32),
            pltpu.VMEM((2, 8, 2, 8, 128), f32),
            dma, dma((4,)),
            dma((3,)), dma((3,)), dma((3,)), dma((3,)),
            dma((2, 7, 2, parts)), dma((2, 7, 2, parts)), dma((2, 7)), dma((2, 7)),
        ],
        compiler_params=pltpu.CompilerParams(
            collective_id=0, has_side_effects=True, vmem_limit_bytes=52 << 20
        ),
        name="project",
    )(lens, norm_gain.reshape(1, shard), qkv_bias.reshape(1, -1), qkv_weight, tokens)


def turn_plain(joined, lens):
    count = joined.shape[0]
    half = HEAD_DIM // 2
    pos = jnp.arange(count, dtype=jnp.int32) - starts(lens, count)
    freqs = jnp.exp(-(jnp.arange(half, dtype=jnp.float32) * 2.0 / HEAD_DIM) * math.log(1000000.0))
    angle = pos.astype(jnp.float32)[:, None] * freqs[None, :]
    cosine = jnp.tile(jnp.cos(angle), (1, 2))[:, None, :]
    sine = jnp.tile(jnp.sin(angle), (1, 2))[:, None, :]
    heads = joined.reshape(count, GROUP + 2, HEAD_DIM)
    spun = jnp.concatenate([-heads[..., half:], heads[..., :half]], axis=-1)
    turned = (heads * cosine + spun * sine)[:, : GROUP + 1]
    both = jnp.concatenate([turned, heads[:, GROUP + 1 :]], axis=1)
    return both.reshape(count, -1).astype(jnp.bfloat16)


def project_plain(tokens, norm_gain, qkv_weight, qkv_bias):
    tp_count = lax.axis_size("tp")
    req_count = lax.axis_size("req")
    tp_place = lax.axis_index("tp")
    gain_full, bias_full = (
        lax.all_gather(norm_gain.astype(jnp.bfloat16), ("req", "tp"), axis=0, tiled=True),
        lax.all_gather(qkv_bias.astype(jnp.bfloat16), ("req", "tp"), axis=0, tiled=True),
    )
    width = bias_full.shape[0] // tp_count
    bias_block = lax.dynamic_slice_in_dim(bias_full, tp_place * width, width).astype(jnp.float32)
    normed = normalize(tokens, gain_full)
    weight_b = qkv_weight.astype(jnp.bfloat16)
    count = tokens.shape[0]
    gathered = lax.all_gather(weight_b, "req", axis=0, tiled=True)
    regrouped = lax.all_to_all(gathered, "tp", split_axis=1, concat_axis=0, tiled=True)
    shard_rows = weight_b.shape[0]
    reordered = (
        normed.reshape(count, req_count, tp_count, shard_rows)
        .transpose(0, 2, 1, 3)
        .reshape(count, -1)
    )
    joined = jnp.dot(reordered, regrouped, preferred_element_type=jnp.float32)
    return joined + bias_block[None, :]


def shards(small, tokens, norm_gain, qkv_weight, qkv_bias, lengths):
    if small:
        qkv = project(tokens, norm_gain, qkv_weight, qkv_bias, lengths)
    else:
        qkv = turn_plain(project_plain(tokens, norm_gain, qkv_weight, qkv_bias), lengths[0])
    return attend_turned(qkv, lengths)


def solution(mesh):
    placed = (
        P("req", None),
        P(("req", "tp")),
        P(("req", "tp"), None),
        P(("req", "tp")),
        P("req", None),
    )
    small = mesh.shape["req"] == 8 and mesh.shape["tp"] == 4
    return jax.shard_map(
        functools.partial(shards, small),
        mesh=mesh, in_specs=placed, out_specs=P("req", "tp"), check_vma=False,
    )
```

```python
import functools
import math

import jax
import jax.numpy as jnp
from jax import lax
from jax.experimental import pallas as pl
from jax.experimental.pallas import tpu as pltpu
from jax.sharding import PartitionSpec as P

HEAD_DIM = 128
SINKS = 4
GROUP = 7
WINDOW = 160
MOST = 256
MESH = pl.DeviceIdType.MESH


def normalize(values, gain):
    wide = values.astype(jnp.float32)
    meansq = jnp.mean(wide * wide, axis=-1, keepdims=True)
    return (wide * lax.rsqrt(meansq + 1e-06) * gain.astype(jnp.float32)).astype(jnp.bfloat16)


def starts(lens, count):
    index = jnp.arange(count, dtype=jnp.int32)
    after = index[:, None] >= jnp.cumsum(lens)[None, :]
    return jnp.sum(jnp.where(after, lens[None, :], 0), axis=1)


def rotated(v, cosine, sine):
    return (v * cosine + pltpu.roll(v, HEAD_DIM // 2, 1) * sine).astype(jnp.bfloat16)


def start_of(query_at, lens_ref):
    start, end = jnp.zeros_like(query_at), jnp.int32(0)
    for t in range(lens_ref.shape[1]):
        end = end + lens_ref[0, t]
        start = jnp.where(query_at >= end, end, start)
    return start


def attend_kernel(lens_ref, qkv_ref, out_ref):
    count = qkv_ref.shape[0]
    block = 128
    back = -(-(MOST - 1) // block)
    for at in range(count // block):
        first = max(0, at - back)
        wide = (at + 1 - first) * block
        rows = slice(at * block, (at + 1) * block)
        seen = slice(first * block, (at + 1) * block)
        query_at = at * block + lax.broadcasted_iota(jnp.int32, (block, 1), 0)
        key_at = first * block + lax.broadcasted_iota(jnp.int32, (block, wide), 1)
        start = start_of(query_at, lens_ref)
        low = jnp.maximum(query_at - (WINDOW - 1), start)
        allowed = jnp.logical_and(
            key_at <= query_at,
            jnp.logical_or(
                key_at >= low, jnp.logical_and(key_at >= start, key_at < start + SINKS)
            ),
        )
        query = jnp.concatenate(
            [qkv_ref[rows, h * HEAD_DIM : (h + 1) * HEAD_DIM] for h in range(GROUP)], axis=0
        )
        scores = lax.dot_general(
            query, qkv_ref[seen, GROUP * HEAD_DIM : (GROUP + 1) * HEAD_DIM],
            (((1,), (1,)), ((), ())), preferred_element_type=jnp.float32,
        ) * (1.0 / math.sqrt(HEAD_DIM))
        scores = jnp.where(allowed[None], scores.reshape(GROUP, block, wide), -1e30)
        peak = jnp.max(scores, axis=-1, keepdims=True)
        expo = jnp.exp(scores - peak)
        weights = (expo * (1.0 / jnp.sum(expo, axis=-1, keepdims=True))).astype(jnp.bfloat16)
        mixed = jnp.dot(
            weights.reshape(GROUP * block, wide), qkv_ref[seen, (GROUP + 1) * HEAD_DIM :],
            preferred_element_type=jnp.float32,
        ).astype(jnp.bfloat16)
        for h in range(GROUP):
            out_ref[rows, h * HEAD_DIM : (h + 1) * HEAD_DIM] = mixed[h * block : (h + 1) * block]


def attend_turned(qkv, lens):
    count = qkv.shape[0]
    vmem = pl.BlockSpec(memory_space=pltpu.VMEM)
    return pl.pallas_call(
        attend_kernel,
        out_shape=jax.ShapeDtypeStruct((count, GROUP * HEAD_DIM), jnp.bfloat16),
        in_specs=[pl.BlockSpec(memory_space=pltpu.SMEM), vmem],
        out_specs=vmem,
        compiler_params=pltpu.CompilerParams(vmem_limit_bytes=64 << 20),
        name="attention",
    )(lens, qkv)


def project_kernel(
    cuts, lens_hbm, gain_hbm, bias_hbm, w_hbm, tok_hbm, out_ref,
    lens_ref, gain_ref, bias_ref, small_sem, wide_w, wb, full, tok, pieces, scale, total, cosine, sine, side, sides,
    tok_sem, w_sem, first_send, first_recv, side_send, side_recv,
    ring_send, ring_recv, trail_send, trail_recv,
):
    req, tp = lax.axis_index("req"), lax.axis_index("tp")
    count, depth = tok.shape
    shard = wb.shape[1]
    width = full.shape[2]
    z, x = req // 2, req % 2
    y, core = tp // 2, tp % 2
    place = (1 - x) * z + x * (7 - z)

    def req_at(pos):
        pos = pos % 8
        far = pos // 4
        return (1 - far) * (2 * pos) + far * (2 * (7 - pos) + 1)

    right, left = req_at(place + 1), req_at(place + 7)
    peers = (2 * y + 1 - core, 2 * (1 - y) + core, 2 * (1 - y) + 1 - core)
    own = 4 * req + tp

    barrier = pltpu.get_barrier_semaphore()
    for peer in peers:
        pl.semaphore_signal(barrier, inc=1, device_id=(req, peer), device_id_type=MESH)
    for near in (left, right):
        pl.semaphore_signal(barrier, inc=1, device_id=(near, tp), device_id_type=MESH)

    smalls = [
        pltpu.make_async_copy(source, to, small_sem.at[k])
        for k, (source, to) in enumerate(
            ((gain_hbm, gain_ref), (bias_hbm, bias_ref), (lens_hbm, lens_ref))
        )
    ]
    for copy in smalls:
        copy.start()
    loads = []
    for k, t in enumerate(peers + (tp,)):
        copy = pltpu.make_async_copy(
            w_hbm.at[:, pl.ds(pl.multiple_of(t * width, 128), width)], wide_w.at[k], w_sem.at[k]
        )
        loads.append(copy)
    for k in (0, 3, 1, 2):
        loads[k].start()
    tok_copy = pltpu.make_async_copy(tok_hbm, tok, tok_sem)
    tok_copy.start()

    def rounded(v):
        return v.astype(jnp.bfloat16).astype(jnp.float32)

    for copy in smalls:
        copy.wait()
    side[...] = jnp.zeros_like(side)
    side[0:1, 0:shard] = rounded(gain_ref[...])
    side[1:2, :] = rounded(bias_ref[:, 0:128])
    side[2:3, 0 : width // 8 - 128] = rounded(bias_ref[:, 128:])

    pl.semaphore_wait(barrier, 5)
    side_firsts = []
    for k, peer in enumerate(peers):
        copy = pltpu.make_async_remote_copy(
            src_ref=side, dst_ref=sides.at[core, req, y],
            send_sem=side_send.at[k], recv_sem=side_recv.at[k],
            device_id=(req, peer), device_id_type=MESH,
        )
        copy.start()
        side_firsts.append(copy)
    sides[core, req, y] = side[...]
    firsts = {}
    for k in (0, 3, 1, 2):
        loads[k].wait()
        if k == 3:
            full[own, 0:shard, :] = wide_w[k].astype(jnp.bfloat16)
            continue
        wb[k] = wide_w[k].astype(jnp.bfloat16)
        copy = pltpu.make_async_remote_copy(
            src_ref=wb.at[k], dst_ref=full.at[own, pl.ds(0, shard)],
            send_sem=first_send.at[k], recv_sem=first_recv.at[k],
            device_id=(req, peers[k]), device_id_type=MESH,
        )
        copy.start()
        firsts[k] = copy

    ring = {}
    trail = {}

    def source_of(way, hop):
        return req_at(place + 8 - hop) if way == 0 else req_at(place + hop)

    def slot_of(way, hop, piece):
        row = y if piece == 0 else 1 - y
        return 4 * source_of(way, hop) + 2 * row + way

    def send(way, hop, piece, part):
        rows = full.at[slot_of(way, hop, piece), pl.ds(cuts[part], cuts[part + 1] - cuts[part])]
        copy = pltpu.make_async_remote_copy(
            src_ref=rows, dst_ref=rows,
            send_sem=ring_send.at[way, hop, piece, part],
            recv_sem=ring_recv.at[way, hop, piece, part],
            device_id=(right if way == 0 else left, tp), device_id_type=MESH,
        )
        copy.start()
        ring[way, hop, piece, part] = copy

    def send_trail(way, hop):
        block = sides.at[way, source_of(way, hop)]
        copy = pltpu.make_async_remote_copy(
            src_ref=block, dst_ref=block,
            send_sem=trail_send.at[way, hop], recv_sem=trail_recv.at[way, hop],
            device_id=(right if way == 0 else left, tp), device_id_type=MESH,
        )
        copy.start()
        trail[way, hop] = copy

    def place_pieces(quarter):
        group = depth // 4
        base = quarter * group

        @pl.loop(0, count // 64)
        def _(i):
            rows = pl.ds(pl.multiple_of(i * 64, 64), 64)
            for k in range(8):
                lo = base + shard * k
                at = lo // 128 * 128
                span = tok[rows, at : min(at + 256, depth)].astype(jnp.float32)
                size = span.shape[1]
                if lo > at:
                    span = pltpu.roll(span, size - (lo - at), 1)
                lane = lax.broadcasted_iota(jnp.int32, (64, 128), 1)
                part = jnp.where(lane < shard, span[:, 0:128], 0.0)
                pieces[8 * quarter + k, rows, :] = part.astype(jnp.bfloat16)

    def factor(slot, way):
        gain = sides[way, slot // 4, slot % 4 // 2, 0:1, :]
        return (pieces[slot].astype(jnp.float32) * scale[...] * gain).astype(jnp.bfloat16)

    def factors(hop, piece):
        return jnp.concatenate(
            [factor(slot_of(way, hop, piece), way) for way in range(2)], axis=1
        )

    def blocks(hop, piece, columns):
        return jnp.concatenate(
            [full[slot_of(way, hop, piece), :, columns] for way in range(2)], axis=0
        )

    def multiply(hop, piece, begin=False):
        lhs = factors(hop, piece)
        for n in range(3):
            part = slice(n * (width // 3), (n + 1) * (width // 3))
            product = jnp.dot(lhs, blocks(hop, piece, part), preferred_element_type=jnp.float32)
            if begin:
                total[:, part] = product
            else:
                total[:, part] += product

    due = {
        3: ((0, 1),),
        4: ((1, 0), (2, 0), (1, 1)),
        5: ((3, 0), (2, 1), (4, 0)),
        6: ((5, 0), (3, 1), (4, 1), (6, 0)),
        7: ((5, 1), (7, 0), (6, 1)),
    }
    parts = len(cuts) - 1
    for step in range(8):
        if step == 0:
            firsts[0].wait_recv()
        for part in range(parts):
            for way in range(2):
                if step >= 1:
                    ring[way, step - 1, 0, part].wait_recv()
                if step <= 6:
                    send(way, step, 0, part)
        if step == 0:
            for copy in side_firsts:
                copy.wait_recv()
        for way in range(2):
            if step >= 1:
                trail[way, step - 1].wait_recv()
            if step <= 6:
                send_trail(way, step)
        if step == 1:
            firsts[1].wait_recv()
            firsts[2].wait_recv()
        if step >= 1:
            for part in range(parts):
                for way in range(2):
                    if step >= 2:
                        ring[way, step - 2, 1, part].wait_recv()
                    send(way, step - 1, 1, part)
        if step == 0:
            @pl.loop(0, full.shape[0])
            def _(i):
                full[i, shard:, :] = jnp.zeros((full.shape[1] - shard, width), jnp.bfloat16)

            tok_copy.wait()

            @pl.loop(0, count // 32)
            def _(i):
                rows = pl.ds(pl.multiple_of(i * 32, 32), 32)
                wide = tok[rows, :].astype(jnp.float32)
                mean = jnp.sum(wide * wide, axis=-1, keepdims=True) * (1.0 / depth)
                scale[rows, :] = jnp.broadcast_to(lax.rsqrt(mean + 1e-06), (32, 128))
        elif step == 1:
            place_pieces(0)
            place_pieces(1)
        elif step == 2:
            place_pieces(2)
            place_pieces(3)
        elif step == 3:
            at = lax.broadcasted_iota(jnp.int32, (count, 1), 0)
            pos = (at - start_of(at, lens_ref)).astype(jnp.float32)
            lane = lax.broadcasted_iota(jnp.int32, (1, HEAD_DIM), 1)
            half = HEAD_DIM // 2
            freqs = jnp.exp(
                -((lane % half).astype(jnp.float32) * 2.0 / HEAD_DIM) * math.log(1000000.0)
            )
            angle = pos * freqs
            cosine[...] = jnp.cos(angle)
            sine[...] = jnp.where(lane < half, -1.0, 1.0) * jnp.sin(angle)
            multiply(0, 0, True)
        for distance, piece in due.get(step, ()):
            multiply(distance, piece)
    lines = [
        sides[(8 * tp + i) % 2, (8 * tp + i) // 4, (8 * tp + i) % 4 // 2] for i in range(8)
    ]
    bias = jnp.zeros((8, width), jnp.float32)
    for i, both in enumerate(lines):
        line = jnp.concatenate(
            [
                pltpu.roll(both, 7, 0), pltpu.roll(both, 6, 0),
                jnp.zeros((8, width - 256), jnp.float32),
            ],
            axis=1,
        )
        bias = bias + (pltpu.roll(line, width // 8 * i, 1) if i else line)
    bias = bias[0:1, :]
    lhs = factors(7, 1)
    for part in range(parts):
        for way in range(2):
            ring[way, 6, 1, part].wait_recv()
    for n in range(3):
        lo = n * (width // 3)
        part = slice(lo, lo + width // 3)
        product = jnp.dot(lhs, blocks(7, 1, part), preferred_element_type=jnp.float32)
        joined = total[:, part] + product + bias[:, part]
        for k in range(3):
            head = 3 * n + k
            v = joined[:, k * HEAD_DIM : (k + 1) * HEAD_DIM]
            out_ref[:, head * HEAD_DIM : (head + 1) * HEAD_DIM] = (
                rotated(v, cosine[...], sine[...]) if head <= GROUP else v.astype(jnp.bfloat16)
            )
    for copy in (
        list(firsts.values()) + side_firsts + list(ring.values()) + list(trail.values())
    ):
        copy.wait_send()


def project(tokens, norm_gain, qkv_weight, qkv_bias, lens):
    count, depth = tokens.shape
    shard, columns = qkv_weight.shape
    width = columns // 4
    half = shard // 32 * 16
    cuts = (0, shard - half, shard)
    parts = len(cuts) - 1
    vmem = pl.BlockSpec(memory_space=pltpu.VMEM)
    hbm = pl.BlockSpec(memory_space=pltpu.HBM)
    dma = pltpu.SemaphoreType.DMA
    f32, bf16 = jnp.float32, jnp.bfloat16
    return pl.pallas_call(
        functools.partial(project_kernel, cuts),
        out_shape=jax.ShapeDtypeStruct((count, width), bf16),
        in_specs=[hbm] * 5,
        out_specs=vmem,
        scratch_shapes=[
            pltpu.SMEM(lens.shape, jnp.int32),
            pltpu.VMEM((1, shard), f32),
            pltpu.VMEM((1, columns // 32), f32),
            dma((3,)),
            pltpu.VMEM((4, shard, width), f32),
            pltpu.VMEM((3, shard, width), bf16),
            pltpu.VMEM((32, 128, width), bf16),
            pltpu.VMEM((count, depth), bf16),
            pltpu.VMEM((32, count, 128), bf16),
            pltpu.VMEM((count, 128), f32),
            pltpu.VMEM((count, width), f32),
            pltpu.VMEM((count, HEAD_DIM), f32),
            pltpu.VMEM((count, HEAD_DIM), f32),
            pltpu.VMEM((8, 128), f32),
            pltpu.VMEM((2, 8, 2, 8, 128), f32),
            dma, dma((4,)),
            dma((3,)), dma((3,)), dma((3,)), dma((3,)),
            dma((2, 7, 2, parts)), dma((2, 7, 2, parts)), dma((2, 7)), dma((2, 7)),
        ],
        compiler_params=pltpu.CompilerParams(
            collective_id=0, has_side_effects=True, vmem_limit_bytes=64 << 20
        ),
        name="project",
    )(lens, norm_gain.reshape(1, shard), qkv_bias.reshape(1, -1), qkv_weight, tokens)


def turn_plain(joined, lens):
    count = joined.shape[0]
    half = HEAD_DIM // 2
    pos = jnp.arange(count, dtype=jnp.int32) - starts(lens, count)
    freqs = jnp.exp(-(jnp.arange(half, dtype=jnp.float32) * 2.0 / HEAD_DIM) * math.log(1000000.0))
    angle = pos.astype(jnp.float32)[:, None] * freqs[None, :]
    cosine = jnp.tile(jnp.cos(angle), (1, 2))[:, None, :]
    sine = jnp.tile(jnp.sin(angle), (1, 2))[:, None, :]
    heads = joined.reshape(count, GROUP + 2, HEAD_DIM)
    spun = jnp.concatenate([-heads[..., half:], heads[..., :half]], axis=-1)
    turned = (heads * cosine + spun * sine)[:, : GROUP + 1]
    both = jnp.concatenate([turned, heads[:, GROUP + 1 :]], axis=1)
    return both.reshape(count, -1).astype(jnp.bfloat16)


def project_plain(tokens, norm_gain, qkv_weight, qkv_bias):
    tp_count = lax.axis_size("tp")
    req_count = lax.axis_size("req")
    tp_place = lax.axis_index("tp")
    gain_full, bias_full = (
        lax.all_gather(norm_gain.astype(jnp.bfloat16), ("req", "tp"), axis=0, tiled=True),
        lax.all_gather(qkv_bias.astype(jnp.bfloat16), ("req", "tp"), axis=0, tiled=True),
    )
    width = bias_full.shape[0] // tp_count
    bias_block = lax.dynamic_slice_in_dim(bias_full, tp_place * width, width).astype(jnp.float32)
    normed = normalize(tokens, gain_full)
    weight_b = qkv_weight.astype(jnp.bfloat16)
    count = tokens.shape[0]
    gathered = lax.all_gather(weight_b, "req", axis=0, tiled=True)
    regrouped = lax.all_to_all(gathered, "tp", split_axis=1, concat_axis=0, tiled=True)
    shard_rows = weight_b.shape[0]
    reordered = (
        normed.reshape(count, req_count, tp_count, shard_rows)
        .transpose(0, 2, 1, 3)
        .reshape(count, -1)
    )
    joined = jnp.dot(reordered, regrouped, preferred_element_type=jnp.float32)
    return joined + bias_block[None, :]


def shards(small, tokens, norm_gain, qkv_weight, qkv_bias, lengths):
    if small:
        qkv = project(tokens, norm_gain, qkv_weight, qkv_bias, lengths)
    else:
        qkv = turn_plain(project_plain(tokens, norm_gain, qkv_weight, qkv_bias), lengths[0])
    return attend_turned(qkv, lengths)


def solution(mesh):
    placed = (
        P("req", None),
        P(("req", "tp")),
        P(("req", "tp"), None),
        P(("req", "tp")),
        P("req", None),
    )
    small = mesh.shape["req"] == 8 and mesh.shape["tp"] == 4
    return jax.shard_map(
        functools.partial(shards, small),
        mesh=mesh, in_specs=placed, out_specs=P("req", "tp"), check_vma=False,
    )
```
